128 devices in a mesh: grp: 16 (over x, y), dev: 8 (over z, core).
Axes of the slice: x: 4, y: 4, z: 4, core: 2. Of those that a mesh axis runs over, the one named last changes fastest.
Arguments:
- queries: bfloat16 [16384, 4096], P(('grp', 'dev')), may hold values from -2 to 2
- passages: bfloat16 [16384, 4096], P(('grp', 'dev')), may hold values from -2 to 2
- destination: int32 [16384, 1], P(('grp', 'dev')), may hold values from 0 to 127; in each aligned block of 128 rows (0 to 127, 128 to 255, ...) at most 2 rows name the same one
Outputs:
- query_grads: bfloat16 [16384, 4096], P(('grp', 'dev'))
- passage_grads: bfloat16 [16384, 4096], P(('grp', 'dev'))
The draws below stay inside these ranges and needn't reach their ends.
Inputs may be any that keep to these rules, and one draw needn't show every extreme that they name: The pairs of one device send at most 2 pairs to one destination device, and exactly 2 in some device.
All inputs are finite; a program needn't handle non-finite values.
Results may differ from the reference program's by a relative error of at most 0.008.
Values may be sent and summed in bfloat16 or wider, within the bound.
A program may use at most 128 MiB of HBM per device.

```python
import math
import jax
import jax.numpy as jnp
import numpy as np
from jax import lax

D = 4096
PAIRS_DEV = 128
TOKENS = 16384
CAP = 2
SLOTS = 256
N_GRP = 16
N_DEV = 8
DEVICES = 128


def pair_draw(key):
    keys = jax.random.split(jax.random.fold_in(key, 11), 2)
    shape = (TOKENS, D)
    passages = jnp.clip(jax.random.normal(keys[0], shape, jnp.float32), -6.0, 6.0)
    queries = jnp.clip(jax.random.normal(keys[1], shape, jnp.float32), -6.0, 6.0)
    norm_scale = 1.0 / jnp.sqrt(jnp.float32(D))
    return (queries * norm_scale, passages * norm_scale)


def draw_queries(key, part):
    return pair_draw(key)[0].astype(jnp.bfloat16)


def draw_passages(key, part):
    return pair_draw(key)[1].astype(jnp.bfloat16)


def shared_out(own_key, own, number, rows, number_of, top, bound, skew):
    ranking = jax.random.permutation(own_key, number_of)
    heavy_load, common = portions_of(number_of, rows * top, bound, skew, True), portions_of(number_of, rows * top, bound, skew, False)
    places = jnp.arange(number_of)

    def named(tallies, turn):
        used = int((tallies > 0).sum())
        fixed = max(1, used // 4)
        shifted = fixed + (places - fixed + turn * (used - fixed)) % max(1, number_of - fixed)
        return jnp.zeros((number_of,), jnp.int32).at[ranking[jnp.where(places < fixed, places, shifted)]].set(jnp.asarray(tallies, jnp.int32))

    tallies = jnp.where(number % 4 == 0, named(heavy_load, number // 4), named(common, number - number // 4 - 1))
    mixed = jax.random.permutation(jax.random.fold_in(own, 3), number_of)
    source_of, taker = mixed[0:number_of // 2 * 2:2], mixed[1:number_of // 2 * 2:2]
    slack = jnp.minimum(tallies[source_of] - 1, bound - tallies[taker]) // 2
    slack = jnp.where((source_of == ranking[0]) | (taker == ranking[0]) | (tallies[taker] == 0), 0, jnp.maximum(slack, 0))
    shifted = jax.random.randint(jax.random.fold_in(own, 4), (number_of // 2,), 0, 1 << 20) % (slack + 1)
    tallies = tallies.at[source_of].add(-shifted).at[taker].add(shifted)
    items = jnp.searchsorted(jnp.cumsum(tallies), jnp.arange(rows * top), side="right").astype(jnp.int32)
    table = items.reshape(top, rows).T
    table = table[jax.random.permutation(jax.random.fold_in(own, 1), rows)]
    turn = jax.random.randint(jax.random.fold_in(own, 2), (rows, 1), 0, top)
    return jnp.take_along_axis(table, (jnp.arange(top)[None, :] + turn) % top, axis=1)


def portions_of(count, total, limit, skew, full):
    loads = [(1 << 20) // math.isqrt(grade ** skew) + 1 for grade in range(1, count + 1)]
    largest = limit if full else min(limit, max(-(-total // count), total * loads[0] // sum(loads)))
    least = 1 if total - largest >= count - 1 else 0
    counts, rest = [largest] + [least] * (count - 1), total - largest - least * (count - 1)
    while rest > 0:
        free = [i for i in range(1, count) if counts[i] < largest] or [i for i in range(1, count) if counts[i] < limit]
        whole, left = sum([loads[i] for i in free]), rest
        for i in free:
            more = min(limit - counts[i], max(1, left * loads[i] // whole), rest)
            counts[i] = counts[i] + more
            rest = rest - more
    return np.array(counts)


def setup_inputs(seed: int = 0) -> dict:
    splits = jax.random.split(jax.random.key(seed), 4)
    queries = draw_queries(jax.random.fold_in(splits[3], 71), 0)
    passages = draw_passages(jax.random.fold_in(splits[3], 71), 0)
    destination_keys = jax.random.split(jax.random.fold_in(splits[2], 1), TOKENS // PAIRS_DEV)
    destination_turns = jax.random.permutation(jax.random.fold_in(splits[2], 3), TOKENS // PAIRS_DEV)
    destination = jax.vmap(lambda own, number: shared_out(jax.random.fold_in(splits[2], 2), own, number, PAIRS_DEV, DEVICES, 1, CAP, 2))(destination_keys, destination_turns).reshape((TOKENS, 1))
    return {"queries": queries, "passages": passages, "destination": destination}


inverse_temp = 100.0


def reference(queries, passages, destination):
    dest_flat = destination[:, 0].astype(jnp.int32)
    per_device = dest_flat.reshape(DEVICES, PAIRS_DEV)
    row_order = jnp.arange(PAIRS_DEV)
    earlier = row_order[None, :] < row_order[:, None]
    rank_index = jnp.sum(((per_device[:, :, None] == per_device[:, None, :]) & earlier[None]).astype(jnp.int32), axis=2)
    source_id = jnp.arange(DEVICES, dtype=jnp.int32)[:, None]
    slot_place = ((per_device % N_DEV) * SLOTS + source_id * CAP + rank_index).reshape(-1).astype(jnp.int32)
    group_of = (dest_flat // N_DEV).astype(jnp.int32)
    group_width = N_DEV * SLOTS

    def one_group(group_id):
        place_at = jnp.where(group_of == group_id, slot_place, group_width)
        q_grp = jnp.zeros((group_width, D), jnp.bfloat16).at[place_at].set(queries, mode="drop")
        p_grp = jnp.zeros((group_width, D), jnp.bfloat16).at[place_at].set(passages, mode="drop")
        filled = jnp.zeros((group_width,), jnp.float32).at[place_at].set(1.0, mode="drop")
        scores = inverse_temp * jnp.dot(q_grp, p_grp.T, preferred_element_type=jnp.float32)
        scores = jnp.where(filled[None, :] > 0, scores, -1e30)
        row_max = jnp.max(scores, axis=1, keepdims=True)
        exp_scores = jnp.exp(scores - row_max)
        softmax_bf = (exp_scores / jnp.sum(exp_scores, axis=1, keepdims=True) * filled[:, None]).astype(jnp.bfloat16)
        query_grad = (inverse_temp * (jnp.dot(softmax_bf, p_grp, preferred_element_type=jnp.float32)
                                      - filled[:, None] * p_grp.astype(jnp.float32))).astype(jnp.bfloat16)
        soft_blocks = softmax_bf.reshape(N_DEV, SLOTS, group_width)
        q_blocks = q_grp.reshape(N_DEV, SLOTS, D)
        fill_blocks = filled.reshape(N_DEV, SLOTS)

        def add_block(member_id, total):
            soft_one = lax.dynamic_index_in_dim(soft_blocks, member_id, 0, keepdims=False)
            q_one = lax.dynamic_index_in_dim(q_blocks, member_id, 0, keepdims=False)
            fill_one = lax.dynamic_index_in_dim(fill_blocks, member_id, 0, keepdims=False)
            block_term = lax.dot_general(soft_one, q_one, (((0,), (0,)), ((), ())), preferred_element_type=jnp.float32)
            own_rows = jnp.zeros((group_width, D), jnp.float32)
            own_rows = lax.dynamic_update_slice_in_dim(own_rows, fill_one[:, None] * q_one.astype(jnp.float32),
                                                       (member_id * SLOTS).astype(jnp.int32), 0)
            rounded = lax.optimization_barrier((inverse_temp * (block_term - own_rows)).astype(jnp.bfloat16))
            return total + rounded.astype(jnp.float32)

        passage_sum = lax.fori_loop(0, N_DEV, add_block, jnp.zeros((group_width, D), jnp.float32))
        return query_grad, passage_sum.astype(jnp.bfloat16)

    q_all, p_all = lax.map(one_group, jnp.arange(N_GRP, dtype=jnp.int32))
    flat_index = group_of * group_width + slot_place
    return q_all.reshape(-1, D)[flat_index], p_all.reshape(-1, D)[flat_index]
```

```python
import functools

import jax
import jax.numpy as jnp
from jax import lax
from jax.experimental import pallas as pl
from jax.experimental.pallas import tpu as pltpu
from jax.sharding import PartitionSpec as P

inverse_temp = 100.0
MESH = pl.DeviceIdType.MESH
SEATS = 32
NZ = 4
CHUNKS = 4
F32, BF16 = jnp.float32, jnp.bfloat16


def wait_bytes(ref, sem):
    pltpu.make_async_copy(ref, ref, sem).wait()


def kernel(
    drow_ref, q_ref, p_ref, oq_ref, op_ref,
    dest, xp, xq, place, unplace, pay_p, pay_q, p_all, q_rows, marks_out, marks, valid,
    scores, scores_in, soft, soft_t, dq, t1, t2, t3, ra, rb, rl, rr, dp, back_q, back_p, out_q, out_p,
    swap_s, swap_r, local_s, place_s, place_r, mark_s, mark_r, ring_s, ring_r, core_s, core_r,
    sum_s, sum_r, back_s, back_r, out_s, out_r,
):
    n_group = p_all.shape[2]
    npairs = q_ref.shape[0]
    half_d = q_ref.shape[1] // 2
    width = p_all.shape[4]
    rows = n_group * SEATS
    half_g = n_group // 2
    half = rows // 2
    g = lax.axis_index("grp")
    d = lax.axis_index("dev")
    c = lax.rem(d, 2)
    z = lax.div(d, 2)
    up = lax.rem(z + 1, NZ) * 2 + c
    down = lax.rem(z + NZ - 1, NZ) * 2 + c
    far = lax.rem(z + 2, NZ) * 2 + c
    mate = z * 2 + (1 - c)

    def remote(src, dst, s, r, to):
        return pltpu.make_async_remote_copy(
            src_ref=src, dst_ref=dst, send_sem=s, recv_sem=r, device_id=to, device_id_type=MESH
        )

    mine = pl.ds(pl.multiple_of(c * half_d, half_d), half_d)
    theirs = pl.ds(pl.multiple_of((1 - c) * half_d, half_d), half_d)
    own_copies = [
        pltpu.make_async_copy(drow_ref, dest.at[c], local_s.at[0]),
        pltpu.make_async_copy(p_ref.at[:, mine], xp.at[c], local_s.at[1]),
        pltpu.make_async_copy(q_ref.at[:, mine], xq.at[c], local_s.at[2]),
    ]
    for copy in own_copies:
        copy.start()

    barrier = pltpu.get_barrier_semaphore()
    for to in (up, down, far, mate):
        pl.semaphore_signal(barrier, inc=1, device_id=(g, to), device_id_type=MESH)

    @pl.loop(1, n_group)
    def _(o):
        pl.semaphore_signal(barrier, inc=1, device_id=(lax.rem(g + o, n_group), d), device_id_type=MESH)

    pl.semaphore_wait(barrier, n_group + 3)

    swaps = [
        remote(drow_ref, dest.at[c], swap_s.at[0], swap_r.at[0], (g, mate)),
        remote(p_ref.at[:, theirs], xp.at[c], swap_s.at[1], swap_r.at[1], (g, mate)),
        remote(q_ref.at[:, theirs], xq.at[c], swap_s.at[2], swap_r.at[2], (g, mate)),
    ]
    for copy in swaps:
        copy.start()

    own_copies[0].wait()
    swaps[0].wait_recv()
    n2 = 2 * npairs
    group = jnp.concatenate([dest[0, 0:1, :], dest[1, 0:1, :]], axis=1)
    group = lax.shift_right_logical(group, jnp.full_like(group, 3))
    along = jnp.broadcast_to(group.astype(F32), (n2, n2))
    across = along.T
    i0 = lax.broadcasted_iota(jnp.int32, (n2, n2), 0)
    i1 = lax.broadcasted_iota(jnp.int32, (n2, n2), 1)
    same = along == across
    rank_row = jnp.sum(jnp.where(same & (i0 < i1), 1.0, 0.0), axis=0, keepdims=True)
    rank_col = jnp.sum(jnp.where(same & (i1 < i0), 1.0, 0.0), axis=1, keepdims=True)
    slot_row = (group.astype(F32) * SEATS + rank_row).astype(jnp.int32)
    slot_col = (across[:, 0:1] * SEATS + rank_col).astype(jnp.int32)
    place[...] = jnp.where(
        lax.broadcasted_iota(jnp.int32, (rows, n2), 0) == slot_row, 1.0, 0.0
    ).astype(BF16)
    unplace[...] = jnp.where(
        lax.broadcasted_iota(jnp.int32, (n2, rows), 1) == slot_col, 1.0, 0.0
    ).astype(BF16)
    count = jnp.sum(
        jnp.where(lax.broadcasted_iota(jnp.int32, (n_group, n2), 0) == group, 1.0, 0.0), axis=1, keepdims=True
    ).astype(jnp.int32)
    lane = lax.broadcasted_iota(jnp.int32, (n_group, 128), 1) - lax.rem(g, 4) * SEATS
    flags = jnp.where((lane >= 0) & (lane < count), 1.0, 0.0)
    for i in range(n_group):
        marks_out[i] = jnp.broadcast_to(flags[i : i + 1], (8, 128))

    def send_all(src, dst, s, r):
        @pl.loop(1, n_group)
        def _(o):
            to = lax.rem(g + o, n_group)
            remote(src.at[to], dst.at[g], s, r, (to, d)).start()

    own_copies[1].wait()
    swaps[1].wait_recv()

    def place_p(k):
        cols = slice(k * width, (k + 1) * width)
        x = xp[:, :, cols].reshape(n2, width)
        pay_p[k] = jnp.dot(place[...], x, preferred_element_type=F32).astype(BF16).reshape(n_group, SEATS, width)
        send_all(pay_p.at[k], p_all.at[k, 0], place_s.at[0, k], place_r.at[0, k])
        p_all[k, 0, g] = pay_p[k, g]

    def place_q(k):
        cols = slice(k * width, (k + 1) * width)
        x = xq[:, :, cols].reshape(n2, width)
        pay_q[k] = jnp.dot(place[...], x, preferred_element_type=F32).astype(BF16).reshape(n_group, SEATS, width)
        send_all(pay_q.at[k], q_rows.at[k], place_s.at[1, k], place_r.at[1, k])
        q_rows[k, g] = pay_q[k, g]

    def wait_all(ref, sem):
        wait_bytes(ref.at[pl.ds(0, n_group - 1)], sem)

    place_p(0)
    send_all(marks_out, marks.at[0], mark_s.at[0], mark_r.at[0])
    marks[0, g] = marks_out[g]
    place_p(1)
    own_copies[2].wait()
    swaps[2].wait_recv()
    place_q(0)
    for k in range(2, CHUNKS):
        place_p(k)
        place_q(k - 1)
    place_q(CHUNKS - 1)

    lo, hi = pl.ds(0, half_g), pl.ds(half_g, half_g)

    def ring(k, i):
        own, above, beyond, below = (p_all.at[k, j] for j in range(4))
        src, dst, to = (
            (own.at[lo], below.at[lo], up),
            (own.at[hi], below.at[hi], up),
            (own.at[hi], above.at[hi], down),
            (own.at[lo], above.at[lo], down),
            (below.at[lo], beyond.at[lo], up),
            (above.at[hi], beyond.at[hi], down),
        )[i]
        return remote(src, dst, ring_s.at[k, i], ring_r.at[k, i], (g, to))

    def add_scores(k, j):
        part = lax.dot_general(
            q_rows[k].reshape(rows, width), p_all[k, j].reshape(rows, width),
            (((1,), (1,)), ((), ())), preferred_element_type=F32,
        )
        scores[j] = part if k == 0 else scores[j] + part

    mark_ring = [
        remote(marks.at[0], marks.at[3], mark_s.at[1], mark_r.at[1], (g, up)),
        remote(marks.at[0], marks.at[1], mark_s.at[2], mark_r.at[2], (g, down)),
        remote(marks.at[0], marks.at[2], mark_s.at[3], mark_r.at[3], (g, far)),
    ]

    for step in range(CHUNKS + 1):
        if step < CHUNKS:
            wait_all(p_all.at[step, 0], place_r.at[0, step])
            for i in (0, 2, 1, 3):
                ring(step, i).start()
        if step == 0:
            wait_all(marks.at[0], mark_r.at[0])
            for copy in mark_ring:
                copy.start()
        if step >= 1:
            k = step - 1
            ring(k, 0).wait_recv()
            ring(k, 4).start()
            ring(k, 2).wait_recv()
            ring(k, 5).start()
        if step == 1:
            for copy in mark_ring:
                copy.wait_recv()
            for j in range(NZ):
                pieces = []
                for first in range(0, n_group, 4):
                    flag = marks[j, first, 0:1, :]
                    for i in range(first + 1, min(first + 4, n_group)):
                        flag = flag + marks[j, i, 0:1, :]
                    pieces.append(flag)
                flag = pieces[0] if len(pieces) == 1 else jnp.concatenate(pieces, axis=1)
                valid[j] = jnp.broadcast_to(flag[:, :rows], (8, rows))
        if step >= 2:
            k = step - 2
            wait_all(q_rows.at[k], place_r.at[1, k])
            for i in (1, 3, 4, 5):
                ring(k, i).wait_recv()
            for j in range(NZ):
                add_scores(k, j)

    row_valid = jnp.broadcast_to(valid[0, 0:1, :], (128, rows)).T

    my_rows = pl.ds(pl.multiple_of(c * half, half), half)
    mate_rows = pl.ds(pl.multiple_of((1 - c) * half, half), half)

    def share(j):
        return remote(scores.at[j, mate_rows], scores_in.at[j], core_s.at[j], core_r.at[j], (g, mate))

    last = CHUNKS - 1
    wait_all(q_rows.at[last], place_r.at[1, last])
    for j in (0, 3, 1, 2):
        if j == 3:
            ring(last, 1).wait_recv()
        if j == 1:
            ring(last, 3).wait_recv()
        if j == 2:
            ring(last, 4).wait_recv()
            ring(last, 5).wait_recv()
        add_scores(last, j)
        share(j).start()

    out_q_cols = row_valid
    soft_t[0, :, 0:128] = out_q_cols.astype(BF16)
    for j in range(NZ):
        share(j).wait_recv()

    tile = min(16, half)

    @pl.loop(0, half // tile)
    def _(i):
        at_out = pl.ds(pl.multiple_of(c * half + i * tile, tile), tile)
        at_in = pl.ds(pl.multiple_of(i * tile, tile), tile)
        keep = soft_t[0, at_out, 0:1].astype(F32)
        parts = []
        top = None
        for j in range(NZ):
            s = inverse_temp * (scores[j, at_out, :] + scores_in[j, at_in, :])
            s = jnp.where(valid[j, 0:1, :] > 0, s, -1e30)
            parts.append(s)
            m = jnp.max(s, axis=1, keepdims=True)
            top = m if top is None else jnp.maximum(top, m)
        total = None
        exps = []
        for s in parts:
            e = jnp.exp(s - top)
            exps.append(e)
            t = jnp.sum(e, axis=1, keepdims=True)
            total = t if total is None else total + t
        for j in range(NZ):
            soft[j, at_out, :] = (exps[j] / total * keep).astype(BF16)

    give = remote(soft.at[:, my_rows], soft.at[:, my_rows], core_s.at[NZ], core_r.at[NZ], (g, mate))
    give.start()
    my_lanes = pl.ds(pl.multiple_of(c * half, half), half)
    mate_lanes = pl.ds(pl.multiple_of((1 - c) * half, half), half)
    for j in (2, 1, 3, 0):
        soft_t[j, :, my_lanes] = soft[j, my_rows, :].T
    give.wait_recv()
    for j in (2, 1, 3, 0):
        soft_t[j, :, mate_lanes] = soft[j, mate_rows, :].T

    def q_of(k):
        return q_rows[k].reshape(rows, width)

    def term(k, j, first, size):
        return inverse_temp * jnp.dot(soft_t[j, pl.ds(first, size), :], q_of(k), preferred_element_type=F32)

    a, b = pl.ds(0, half), pl.ds(half, half)

    def summed(k, i):
        src, dst, to = (
            (t2.at[k, a], ra.at[k], up),
            (t2.at[k, b], rb.at[k], down),
            (t1.at[k, b], rl.at[k, b], up),
            (t3.at[k, a], rr.at[k, a], down),
            (t1.at[k, a], rl.at[k, a], up),
            (t3.at[k, b], rr.at[k, b], down),
        )[i]
        return remote(src, dst, sum_s.at[k, i], sum_r.at[k, i], (g, to))

    for step in range(CHUNKS + 2):
        if step < CHUNKS:
            k = step
            t2[k] = term(k, 2, 0, rows).astype(BF16)
            summed(k, 0).start()
            summed(k, 1).start()
            t1[k, b] = term(k, 1, half, half).astype(BF16)
            summed(k, 2).start()
            t3[k, a] = term(k, 3, 0, half).astype(BF16)
            summed(k, 3).start()
        if 1 <= step <= CHUNKS:
            k = step - 1
            summed(k, 0).wait_recv()
            t1[k, a] = (term(k, 1, 0, half) + ra[k].astype(F32)).astype(BF16)
            summed(k, 4).start()
            summed(k, 1).wait_recv()
            t3[k, b] = (term(k, 3, half, half) + rb[k].astype(F32)).astype(BF16)
            summed(k, 5).start()
        if step < CHUNKS:
            k = step
            acc = -p_all[k, 0].reshape(rows, width).astype(F32)
            for j in range(NZ):
                acc = acc + jnp.dot(soft[j], p_all[k, j].reshape(rows, width), preferred_element_type=F32)
            dq[k] = (inverse_temp * acc).astype(BF16).reshape(n_group, SEATS, width)
            send_all(dq.at[k], back_q.at[k], back_s.at[0, k], back_r.at[0, k])
            back_q[k, g] = dq[k, g]
        if step >= 2:
            k = step - 2
            own = inverse_temp * (
                jnp.dot(soft_t[0], q_of(k), preferred_element_type=F32) - q_of(k).astype(F32)
            )
            for i in (2, 3, 4, 5):
                summed(k, i).wait_recv()
            own = own + rl[k].astype(F32) + rr[k].astype(F32)
            dp[k] = own.astype(BF16).reshape(n_group, SEATS, width)
            send_all(dp.at[k], back_p.at[k], back_s.at[1, k], back_r.at[1, k])
            back_p[k, g] = dp[k, g]

    def finish(k, which):
        back, out, o_ref = ((back_q, out_q, oq_ref), (back_p, out_p, op_ref))[which]
        wait_all(back.at[k], back_r.at[which, k])
        out[k] = (
            jnp.dot(unplace[...], back[k].reshape(rows, width), preferred_element_type=F32)
            .astype(BF16)
            .reshape(2, npairs, width)
        )
        here, there = outputs(k, which)
        here.start()
        there.start()

    def outputs(k, which):
        out, o_ref = ((out_q, oq_ref), (out_p, op_ref))[which]
        cols = pl.ds(pl.multiple_of(c * half_d + k * width, width), width)
        return (
            pltpu.make_async_copy(out.at[k, c], o_ref.at[:, cols], local_s.at[3 + which * CHUNKS + k]),
            remote(out.at[k, 1 - c], o_ref.at[:, cols], out_s.at[which, k], out_r.at[which, k], (g, mate)),
        )

    for k in range(CHUNKS):
        finish(k, 0)
    for k in range(CHUNKS):
        finish(k, 1)

    for copy in swaps:
        copy.wait_send()
    for k in range(CHUNKS):
        wait_all(pay_p.at[k], place_s.at[0, k])
        wait_all(pay_q.at[k], place_s.at[1, k])
        wait_all(dq.at[k], back_s.at[0, k])
        wait_all(dp.at[k], back_s.at[1, k])
        for i in range(6):
            ring(k, i).wait_send()
            summed(k, i).wait_send()
    wait_all(marks_out, mark_s.at[0])
    for copy in mark_ring:
        copy.wait_send()
    for j in range(NZ):
        share(j).wait_send()
    give.wait_send()
    for which in range(2):
        for k in range(CHUNKS):
            here, there = outputs(k, which)
            here.wait()
            there.wait()


def local(queries, passages, destination):
    n_group = lax.axis_size("grp")
    npairs, width_d = queries.shape
    half_d = width_d // 2
    width = half_d // CHUNKS
    rows = n_group * SEATS
    half = rows // 2
    drow = jnp.broadcast_to(destination.reshape(1, npairs), (8, npairs))
    dma = pltpu.SemaphoreType.DMA

    def vm(*shape, dtype=BF16):
        return pltpu.VMEM(shape, dtype)

    scratch = [
        vm(2, 8, npairs, dtype=jnp.int32),
        vm(2, npairs, half_d), vm(2, npairs, half_d),
        vm(rows, 2 * npairs), vm(2 * npairs, rows),
        vm(CHUNKS, n_group, SEATS, width), vm(CHUNKS, n_group, SEATS, width),
        vm(CHUNKS, NZ, n_group, SEATS, width), vm(CHUNKS, n_group, SEATS, width),
        vm(n_group, 8, 128, dtype=F32), vm(NZ, n_group, 8, 128, dtype=F32), vm(NZ, 8, rows, dtype=F32),
        vm(NZ, rows, rows, dtype=F32), vm(NZ, half, rows, dtype=F32),
        vm(NZ, rows, rows), vm(NZ, rows, rows),
        vm(CHUNKS, n_group, SEATS, width),
        vm(CHUNKS, rows, width), vm(CHUNKS, rows, width), vm(CHUNKS, rows, width),
        vm(CHUNKS, half, width), vm(CHUNKS, half, width),
        vm(CHUNKS, rows, width), vm(CHUNKS, rows, width),
        vm(CHUNKS, n_group, SEATS, width),
        vm(CHUNKS, n_group, SEATS, width), vm(CHUNKS, n_group, SEATS, width),
        vm(CHUNKS, 2, npairs, width), vm(CHUNKS, 2, npairs, width),
        dma((3,)), dma((3,)), dma((3 + 2 * CHUNKS,)),
        dma((2, CHUNKS)), dma((2, CHUNKS)), dma((4,)), dma((4,)),
        dma((CHUNKS, 6)), dma((CHUNKS, 6)), dma((NZ + 1,)), dma((NZ + 1,)),
        dma((CHUNKS, 6)), dma((CHUNKS, 6)), dma((2, CHUNKS)), dma((2, CHUNKS)),
        dma((2, CHUNKS)), dma((2, CHUNKS)),
    ]
    anywhere = pl.BlockSpec(memory_space=pl.ANY)
    return pl.pallas_call(
        kernel,
        out_shape=(
            jax.ShapeDtypeStruct((npairs, width_d), BF16),
            jax.ShapeDtypeStruct((npairs, width_d), BF16),
        ),
        in_specs=[pl.BlockSpec(memory_space=pltpu.VMEM), anywhere, anywhere],
        out_specs=(anywhere, anywhere),
        scratch_shapes=scratch,
        compiler_params=pltpu.CompilerParams(
            collective_id=0, has_side_effects=True, vmem_limit_bytes=67043328
        ),
    )(drow, queries, passages)


def solution(mesh):
    placed = (P(("grp", "dev"), None), P(("grp", "dev"), None), P(("grp", "dev"), None))
    return jax.shard_map(
        local,
        mesh=mesh,
        in_specs=placed,
        out_specs=(P(("grp", "dev"), None), P(("grp", "dev"), None)),
        check_vma=False,
    )
```

```python
import functools

import jax
import jax.numpy as jnp
from jax import lax
from jax.experimental import pallas as pl
from jax.experimental.pallas import tpu as pltpu
from jax.sharding import PartitionSpec as P

inverse_temp = 100.0
MESH = pl.DeviceIdType.MESH
SEATS = 32
FEW = 24
NZ = 4
CHUNKS = 8
F32, BF16 = jnp.float32, jnp.bfloat16


def wait_bytes(ref, sem):
    pltpu.make_async_copy(ref, ref, sem).wait()


def remote(src, dst, s, r, to):
    return pltpu.make_async_remote_copy(
        src_ref=src, dst_ref=dst, send_sem=s, recv_sem=r, device_id=to, device_id_type=MESH
    )


def where_am_i():
    g = lax.axis_index("grp")
    d = lax.axis_index("dev")
    c = lax.rem(d, 2)
    z = lax.div(d, 2)
    up = lax.rem(z + 1, NZ) * 2 + c
    down = lax.rem(z + NZ - 1, NZ) * 2 + c
    far = lax.rem(z + 2, NZ) * 2 + c
    mate = z * 2 + (1 - c)
    return g, d, c, up, down, far, mate


def greet(n_group):
    g, d, c, up, down, far, mate = where_am_i()
    barrier = pltpu.get_barrier_semaphore()
    for to in (up, down, far, mate):
        pl.semaphore_signal(barrier, inc=1, device_id=(g, to), device_id_type=MESH)

    @pl.loop(1, n_group)
    def _(o):
        pl.semaphore_signal(barrier, inc=1, device_id=(lax.rem(g + o, n_group), d), device_id_type=MESH)

    return lambda: pl.semaphore_wait(barrier, n_group + 3)


def first_kernel(
    drow_ref, q_ref, p_ref, pay_p_ref, pay_q_ref, marks_ref, unplace_ref, top_ref,
    dest, xp, xq, place, pay_p, pay_q, own_top, tops, plane_top, plane_tops,
    swap_s, swap_r, local_s, keep_s, top_s, top_r, plane_s, plane_r,
):
    n_group = pay_p.shape[1]
    npairs = q_ref.shape[0]
    half_d = q_ref.shape[1] // 2
    width = pay_p.shape[3]
    rows = n_group * SEATS
    g, d, c, up, down, far, mate = where_am_i()

    mine = pl.ds(pl.multiple_of(c * half_d, half_d), half_d)
    theirs = pl.ds(pl.multiple_of((1 - c) * half_d, half_d), half_d)
    own_copies = [
        pltpu.make_async_copy(drow_ref, dest.at[c], local_s.at[0]),
        pltpu.make_async_copy(p_ref.at[:, mine], xp.at[c], local_s.at[1]),
        pltpu.make_async_copy(q_ref.at[:, mine], xq.at[c], local_s.at[2]),
    ]
    for copy in own_copies:
        copy.start()
    greet(n_group)()
    swaps = [
        remote(drow_ref, dest.at[c], swap_s.at[0], swap_r.at[0], (g, mate)),
        remote(p_ref.at[:, theirs], xp.at[c], swap_s.at[1], swap_r.at[1], (g, mate)),
        remote(q_ref.at[:, theirs], xq.at[c], swap_s.at[2], swap_r.at[2], (g, mate)),
    ]
    for copy in swaps:
        copy.start()

    own_copies[0].wait()
    swaps[0].wait_recv()
    n2 = 2 * npairs
    group = jnp.concatenate([dest[0, 0:1, :], dest[1, 0:1, :]], axis=1)
    group = lax.shift_right_logical(group, jnp.full_like(group, 3))
    count = jnp.sum(
        jnp.where(lax.broadcasted_iota(jnp.int32, (n_group, n2), 0) == group, 1.0, 0.0), axis=1, keepdims=True
    )
    own_top[...] = jnp.broadcast_to(jnp.max(count, axis=0, keepdims=True), (8, 128))
    tops[g] = own_top[...]

    @pl.loop(1, n_group)
    def _(o):
        to = lax.rem(g + o, n_group)
        remote(own_top, tops.at[g], top_s, top_r, (to, d)).start()

    along = jnp.broadcast_to(group.astype(F32), (n2, n2))
    across = along.T
    i0 = lax.broadcasted_iota(jnp.int32, (n2, n2), 0)
    i1 = lax.broadcasted_iota(jnp.int32, (n2, n2), 1)
    same = along == across
    rank_row = jnp.sum(jnp.where(same & (i0 < i1), 1.0, 0.0), axis=0, keepdims=True)
    rank_col = jnp.sum(jnp.where(same & (i1 < i0), 1.0, 0.0), axis=1, keepdims=True)
    slot_row = (group.astype(F32) * SEATS + rank_row).astype(jnp.int32)
    slot_col = (across[:, 0:1] * SEATS + rank_col).astype(jnp.int32)
    place[...] = jnp.where(
        lax.broadcasted_iota(jnp.int32, (rows, n2), 0) == slot_row, 1.0, 0.0
    ).astype(BF16)
    unplace_ref[...] = jnp.where(
        lax.broadcasted_iota(jnp.int32, (n2, rows), 1) == slot_col, 1.0, 0.0
    ).astype(BF16)
    lane = lax.broadcasted_iota(jnp.int32, (n_group, 128), 1) - lax.rem(g, 4) * SEATS
    flags = jnp.where((lane >= 0) & (lane < count.astype(jnp.int32)), 1.0, 0.0)
    for i in range(n_group):
        marks_ref[i] = jnp.broadcast_to(flags[i : i + 1], (8, 128))

    def fill(x, pay, pay_ref, which):
        @pl.loop(0, CHUNKS)
        def _(k):
            cols = pl.ds(pl.multiple_of(k * width, width), width)
            part = jnp.dot(place[...], x[:, :, cols].reshape(n2, width), preferred_element_type=F32)
            pay[k] = part.astype(BF16).reshape(n_group, SEATS, width)
            pltpu.make_async_copy(pay.at[k], pay_ref.at[k], keep_s.at[which, k]).start()

    own_copies[1].wait()
    swaps[1].wait_recv()
    fill(xp, pay_p, pay_p_ref, 0)

    wait_bytes(tops.at[pl.ds(0, n_group - 1)], top_r)
    top = tops[0]
    for i in range(1, n_group):
        top = jnp.maximum(top, tops[i])
    plane_top[...] = top
    plane_copies = [
        remote(plane_top, plane_tops.at[i], plane_s.at[i], plane_r.at[i], (g, to))
        for i, to in enumerate((up, down, far))
    ]
    for copy in plane_copies:
        copy.start()

    own_copies[2].wait()
    swaps[2].wait_recv()
    fill(xq, pay_q, pay_q_ref, 1)

    for copy in plane_copies:
        copy.wait_recv()
    top_ref[...] = jnp.maximum(
        jnp.maximum(plane_top[...], plane_tops[0]), jnp.maximum(plane_tops[1], plane_tops[2])
    )
    for copy in swaps:
        copy.wait_send()
    for copy in plane_copies:
        copy.wait_send()
    wait_bytes(tops.at[pl.ds(0, n_group - 1)], top_s)

    @pl.loop(0, CHUNKS)
    def _(k):
        pltpu.make_async_copy(pay_p.at[k], pay_p_ref.at[k], keep_s.at[0, k]).wait()
        pltpu.make_async_copy(pay_q.at[k], pay_q_ref.at[k], keep_s.at[1, k]).wait()


def second_kernel(
    seats,
    pay_p, pay_q, marks_out, unplace, oq_ref, op_ref,
    p_all, q_rows, marks, valid, scores, scores_in, soft, soft_t, dq, t1, t2, t3, ra, rb, rl, rr, dp,
    back_q, back_p, out_q, out_p,
    local_s, place_s, place_r, mark_s, mark_r, ring_s, ring_r, core_s, core_r,
    sum_s, sum_r, back_s, back_r, keep_s, out_s, out_r,
):
    n_group = p_all.shape[2]
    npairs, width_d = oq_ref.shape
    half_d = width_d // 2
    width = p_all.shape[4]
    rows = n_group * SEATS
    half_g = n_group // 2
    half = rows // 2
    g, d, c, up, down, far, mate = where_am_i()
    taken = pl.ds(0, seats)

    ready = greet(n_group)
    if seats < SEATS:
        rest = slice(seats, SEATS)
        empty = jnp.zeros((n_group, SEATS - seats, width), BF16)

        @pl.loop(0, CHUNKS)
        def _(k):
            for j in range(NZ):
                p_all[k, j, :, rest, :] = empty
            for ref in (q_rows, back_q, back_p):
                ref[k, :, rest, :] = empty

    ready()

    def send_all(src, dst, s, r):
        @pl.loop(1, n_group)
        def _(o):
            to = lax.rem(g + o, n_group)
            remote(src.at[to, taken], dst.at[g, taken], s, r, (to, d)).start()

    def wait_all(ref, sem):
        wait_bytes(ref.at[pl.ds(0, n_group - 1), taken], sem)

    def send_p(k):
        send_all(pay_p.at[k], p_all.at[k, 0], place_s.at[0, k], place_r.at[0, k])

    own_copies = [
        pltpu.make_async_copy(pay_p.at[:, g, taken], p_all.at[:, 0, g, taken], local_s.at[0]),
        pltpu.make_async_copy(pay_q.at[:, g, taken], q_rows.at[:, g, taken], local_s.at[1]),
        pltpu.make_async_copy(marks_out.at[g], marks.at[0, g], local_s.at[2]),
    ]
    send_p(0)
    for copy in own_copies:
        copy.start()

    @pl.loop(1, n_group)
    def _(o):
        to = lax.rem(g + o, n_group)
        remote(marks_out.at[to], marks.at[0, g], mark_s.at[0], mark_r.at[0], (to, d)).start()

    @pl.loop(1, CHUNKS)
    def _(k):
        send_p(k)

    @pl.loop(0, CHUNKS)
    def _(k):
        send_all(pay_q.at[k], q_rows.at[k], place_s.at[1, k], place_r.at[1, k])

    lo, hi = pl.ds(0, half_g), pl.ds(half_g, half_g)

    def ring(k, i):
        own, above, beyond, below = (p_all.at[k, j] for j in range(4))
        src, dst, part, to = (
            (own, below, lo, up),
            (own, below, hi, up),
            (own, above, hi, down),
            (own, above, lo, down),
            (below, beyond, lo, up),
            (above, beyond, hi, down),
        )[i]
        return remote(src.at[part, taken], dst.at[part, taken], ring_s.at[k, i], ring_r.at[k, i], (g, to))

    def score_part(k, j):
        return lax.dot_general(
            q_rows[k].reshape(rows, width), p_all[k, j].reshape(rows, width),
            (((1,), (1,)), ((), ())), preferred_element_type=F32,
        )

    def start_ring(k):
        wait_all(p_all.at[k, 0], place_r.at[0, k])
        for i in (0, 2, 1, 3):
            ring(k, i).start()

    def pass_on(k):
        ring(k, 0).wait_recv()
        ring(k, 4).start()
        ring(k, 2).wait_recv()
        ring(k, 5).start()

    def add_scores(k):
        wait_all(q_rows.at[k], place_r.at[1, k])
        for i in (1, 3, 4, 5):
            ring(k, i).wait_recv()

        @pl.loop(0, NZ)
        def _(j):
            scores[j] = scores[j] + score_part(k, j)

    mark_ring = [
        remote(marks.at[0], marks.at[3], mark_s.at[1], mark_r.at[1], (g, up)),
        remote(marks.at[0], marks.at[1], mark_s.at[2], mark_r.at[2], (g, down)),
        remote(marks.at[0], marks.at[2], mark_s.at[3], mark_r.at[3], (g, far)),
    ]

    for copy in own_copies:
        copy.wait()
    start_ring(0)
    wait_bytes(marks.at[0, pl.ds(0, n_group - 1)], mark_r.at[0])
    for copy in mark_ring:
        copy.start()
    start_ring(1)
    pass_on(0)
    scores[...] = jnp.zeros_like(scores)
    for copy in mark_ring:
        copy.wait_recv()
    for j in range(NZ):
        pieces = []
        for first in range(0, n_group, 4):
            flag = marks[j, first, 0:1, :]
            for i in range(first + 1, min(first + 4, n_group)):
                flag = flag + marks[j, i, 0:1, :]
            pieces.append(flag)
        flag = pieces[0] if len(pieces) == 1 else jnp.concatenate(pieces, axis=1)
        valid[j] = jnp.broadcast_to(flag[:, :rows], (8, rows))
    soft_t[0, :, 0:128] = jnp.broadcast_to(valid[0, 0:1, :], (128, rows)).T.astype(BF16)

    @pl.loop(2, CHUNKS)
    def _(step):
        start_ring(step)
        pass_on(step - 1)
        add_scores(step - 2)

    pass_on(CHUNKS - 1)
    add_scores(CHUNKS - 2)

    my_rows = pl.ds(pl.multiple_of(c * half, half), half)
    mate_rows = pl.ds(pl.multiple_of((1 - c) * half, half), half)

    def share(j):
        return remote(scores.at[j, mate_rows], scores_in.at[j], core_s.at[j], core_r.at[j], (g, mate))

    last = CHUNKS - 1
    wait_all(q_rows.at[last], place_r.at[1, last])
    for j, needs in ((0, ()), (3, (1,)), (1, (3,)), (2, (4, 5))):
        for i in needs:
            ring(last, i).wait_recv()
        scores[j] = scores[j] + score_part(last, j)
        share(j).start()
    for j in range(NZ):
        share(j).wait_recv()

    tile = min(16, half)

    @pl.loop(0, half // tile)
    def _(i):
        at_out = pl.ds(pl.multiple_of(c * half + i * tile, tile), tile)
        at_in = pl.ds(pl.multiple_of(i * tile, tile), tile)
        keep = soft_t[0, at_out, 0:1].astype(F32)
        parts = []
        top = None
        for j in range(NZ):
            s = inverse_temp * (scores[j, at_out, :] + scores_in[j, at_in, :])
            s = jnp.where(valid[j, 0:1, :] > 0, s, -1e30)
            parts.append(s)
            m = jnp.max(s, axis=1, keepdims=True)
            top = m if top is None else jnp.maximum(top, m)
        total = None
        exps = []
        for s in parts:
            e = jnp.exp(s - top)
            exps.append(e)
            t = jnp.sum(e, axis=1, keepdims=True)
            total = t if total is None else total + t
        for j in range(NZ):
            soft[j, at_out, :] = (exps[j] / total * keep).astype(BF16)

    give = remote(soft.at[:, my_rows], soft.at[:, my_rows], core_s.at[NZ], core_r.at[NZ], (g, mate))
    give.start()
    my_lanes = pl.ds(pl.multiple_of(c * half, half), half)
    mate_lanes = pl.ds(pl.multiple_of((1 - c) * half, half), half)

    @pl.loop(0, NZ)
    def _(j):
        soft_t[j, :, my_lanes] = soft[j, my_rows, :].T

    give.wait_recv()

    @pl.loop(0, NZ)
    def _(j):
        soft_t[j, :, mate_lanes] = soft[j, mate_rows, :].T

    def q_of(k):
        return q_rows[k].reshape(rows, width)

    def term(k, j, first, size):
        return inverse_temp * jnp.dot(soft_t[j, pl.ds(first, size), :], q_of(k), preferred_element_type=F32)

    def blocks(x):
        return x.astype(BF16).reshape(x.shape[0] // SEATS, SEATS, width)

    def summed(k, i):
        src, dst, to = (
            (t2.at[k, lo, taken], ra.at[k, :, taken], up),
            (t2.at[k, hi, taken], rb.at[k, :, taken], down),
            (t1.at[k, hi, taken], rl.at[k, hi, taken], up),
            (t3.at[k, lo, taken], rr.at[k, lo, taken], down),
            (t1.at[k, lo, taken], rl.at[k, lo, taken], up),
            (t3.at[k, hi, taken], rr.at[k, hi, taken], down),
        )[i]
        return remote(src, dst, sum_s.at[k, i], sum_r.at[k, i], (g, to))

    def open_sums(k):
        t2[k] = blocks(term(k, 2, 0, rows))
        summed(k, 0).start()
        summed(k, 1).start()
        t1[k, hi] = blocks(term(k, 1, half, half))
        summed(k, 2).start()
        t3[k, lo] = blocks(term(k, 3, 0, half))
        summed(k, 3).start()

    def add_sums(k):
        summed(k, 0).wait_recv()
        t1[k, lo] = blocks(term(k, 1, 0, half) + ra[k].reshape(half, width).astype(F32))
        summed(k, 4).start()
        summed(k, 1).wait_recv()
        t3[k, hi] = blocks(term(k, 3, half, half) + rb[k].reshape(half, width).astype(F32))
        summed(k, 5).start()

    def query_part(k):
        acc = -p_all[k, 0].reshape(rows, width).astype(F32)
        for j in range(NZ):
            acc = acc + jnp.dot(soft[j], p_all[k, j].reshape(rows, width), preferred_element_type=F32)
        dq[k] = blocks(inverse_temp * acc)
        send_all(dq.at[k], back_q.at[k], back_s.at[0, k], back_r.at[0, k])
        back_q[k, g, 0:seats] = dq[k, g, 0:seats]

    def close_sums(k):
        own = inverse_temp * (
            jnp.dot(soft_t[0], q_of(k), preferred_element_type=F32) - q_of(k).astype(F32)
        )
        for i in (2, 3, 4, 5):
            summed(k, i).wait_recv()
        own = own + rl[k].reshape(rows, width).astype(F32) + rr[k].reshape(rows, width).astype(F32)
        dp[k] = blocks(own)
        send_all(dp.at[k], back_p.at[k], back_s.at[1, k], back_r.at[1, k])
        back_p[k, g, 0:seats] = dp[k, g, 0:seats]

    open_sums(0)
    query_part(0)
    open_sums(1)
    add_sums(0)
    query_part(1)

    @pl.loop(2, CHUNKS)
    def _(k):
        open_sums(k)
        add_sums(k - 1)
        query_part(k)
        close_sums(k - 2)

    add_sums(CHUNKS - 1)
    close_sums(CHUNKS - 2)
    close_sums(CHUNKS - 1)

    def outputs(k, which):
        out, o_ref = ((out_q, oq_ref), (out_p, op_ref))[which]
        cols = pl.ds(pl.multiple_of(c * half_d + k * width, width), width)
        return (
            pltpu.make_async_copy(out.at[k, c], o_ref.at[:, cols], keep_s.at[which, k]),
            remote(out.at[k, 1 - c], o_ref.at[:, cols], out_s.at[which, k], out_r.at[which, k], (g, mate)),
        )

    for which in range(2):
        back, out = ((back_q, out_q), (back_p, out_p))[which]

        @pl.loop(0, CHUNKS)
        def _(k):
            wait_all(back.at[k], back_r.at[which, k])
            part = jnp.dot(unplace[...], back[k].reshape(rows, width), preferred_element_type=F32)
            out[k] = part.astype(BF16).reshape(2, npairs, width)
            here, there = outputs(k, which)
            here.start()
            there.start()

    @pl.loop(0, CHUNKS)
    def _(k):
        wait_all(pay_p.at[k], place_s.at[0, k])
        wait_all(pay_q.at[k], place_s.at[1, k])
        wait_all(dq.at[k], back_s.at[0, k])
        wait_all(dp.at[k], back_s.at[1, k])
        for i in range(6):
            ring(k, i).wait_send()
            summed(k, i).wait_send()
        for which in range(2):
            here, there = outputs(k, which)
            here.wait()
            there.wait()

    wait_bytes(marks_out.at[pl.ds(0, n_group - 1)], mark_s.at[0])
    for copy in mark_ring:
        copy.wait_send()
    for j in range(NZ):
        share(j).wait_send()
    give.wait_send()


def local(queries, passages, destination):
    n_group = lax.axis_size("grp")
    npairs, width_d = queries.shape
    half_d = width_d // 2
    width = half_d // CHUNKS
    rows = n_group * SEATS
    half = rows // 2
    half_g = n_group // 2
    drow = jnp.broadcast_to(destination.reshape(1, npairs), (8, npairs))
    dma = pltpu.SemaphoreType.DMA
    in_vmem = pl.BlockSpec(memory_space=pltpu.VMEM)
    anywhere = pl.BlockSpec(memory_space=pl.ANY)

    def vm(*shape, dtype=BF16):
        return pltpu.VMEM(shape, dtype)

    tile = (8, 128)
    payload = (CHUNKS, n_group, SEATS, width)
    pay_p, pay_q, marks, unplace, top = pl.pallas_call(
        first_kernel,
        out_shape=(
            jax.ShapeDtypeStruct(payload, BF16),
            jax.ShapeDtypeStruct(payload, BF16),
            jax.ShapeDtypeStruct((n_group, *tile), F32),
            jax.ShapeDtypeStruct((2 * npairs, rows), BF16),
            jax.ShapeDtypeStruct(tile, F32),
        ),
        in_specs=[in_vmem, anywhere, anywhere],
        out_specs=(anywhere, anywhere, in_vmem, in_vmem, in_vmem),
        scratch_shapes=[
            vm(2, 8, npairs, dtype=jnp.int32),
            vm(2, npairs, half_d), vm(2, npairs, half_d),
            vm(rows, 2 * npairs),
            vm(*payload), vm(*payload),
            vm(*tile, dtype=F32), vm(n_group, *tile, dtype=F32),
            vm(*tile, dtype=F32), vm(3, *tile, dtype=F32),
            dma((3,)), dma((3,)), dma((3,)), dma((2, CHUNKS)), dma(()), dma(()), dma((3,)), dma((3,)),
        ],
        compiler_params=pltpu.CompilerParams(collective_id=0, has_side_effects=True),
    )(drow, queries, passages)

    def rest(seats, collective_id):
        scratch = [
            vm(CHUNKS, NZ, n_group, SEATS, width), vm(*payload),
            vm(NZ, n_group, *tile, dtype=F32), vm(NZ, 8, rows, dtype=F32),
            vm(NZ, rows, rows, dtype=F32), vm(NZ, half, rows, dtype=F32),
            vm(NZ, rows, rows), vm(NZ, rows, rows),
            vm(*payload),
            vm(*payload), vm(*payload), vm(*payload),
            vm(CHUNKS, half_g, SEATS, width), vm(CHUNKS, half_g, SEATS, width),
            vm(*payload), vm(*payload), vm(*payload),
            vm(*payload), vm(*payload),
            vm(CHUNKS, 2, npairs, width), vm(CHUNKS, 2, npairs, width),
            dma((3,)),
            dma((2, CHUNKS)), dma((2, CHUNKS)), dma((4,)), dma((4,)),
            dma((CHUNKS, 6)), dma((CHUNKS, 6)), dma((NZ + 1,)), dma((NZ + 1,)),
            dma((CHUNKS, 6)), dma((CHUNKS, 6)), dma((2, CHUNKS)), dma((2, CHUNKS)),
            dma((2, CHUNKS)), dma((2, CHUNKS)), dma((2, CHUNKS)),
        ]
        return pl.pallas_call(
            functools.partial(second_kernel, seats),
            out_shape=(
                jax.ShapeDtypeStruct((npairs, width_d), BF16),
                jax.ShapeDtypeStruct((npairs, width_d), BF16),
            ),
            in_specs=[anywhere, anywhere, anywhere, in_vmem],
            out_specs=(anywhere, anywhere),
            scratch_shapes=scratch,
            compiler_params=pltpu.CompilerParams(
                collective_id=collective_id, has_side_effects=True, vmem_limit_bytes=67043328
            ),
        )

    return lax.cond(top[0, 0] <= FEW, rest(FEW, 1), rest(SEATS, 2), pay_p, pay_q, marks, unplace)


def solution(mesh):
    placed = (P(("grp", "dev"), None), P(("grp", "dev"), None), P(("grp", "dev"), None))
    return jax.shard_map(
        local,
        mesh=mesh,
        in_specs=placed,
        out_specs=(P(("grp", "dev"), None), P(("grp", "dev"), None)),
        check_vma=False,
    )
```

```python
import functools

import jax
import jax.numpy as jnp
from jax import lax
from jax.experimental import pallas as pl
from jax.experimental.pallas import tpu as pltpu
from jax.sharding import PartitionSpec as P

inverse_temp = 100.0
MESH = pl.DeviceIdType.MESH
SEATS = 32
FEW = 24
NZ = 4
CHUNKS = 8
F32, BF16 = jnp.float32, jnp.bfloat16


def wait_bytes(ref, sem):
    pltpu.make_async_copy(ref, ref, sem).wait()


def remote(src, dst, s, r, to):
    return pltpu.make_async_remote_copy(
        src_ref=src, dst_ref=dst, send_sem=s, recv_sem=r, device_id=to, device_id_type=MESH
    )


def where_am_i():
    g = lax.axis_index("grp")
    d = lax.axis_index("dev")
    c = lax.rem(d, 2)
    z = lax.div(d, 2)
    up = lax.rem(z + 1, NZ) * 2 + c
    down = lax.rem(z + NZ - 1, NZ) * 2 + c
    far = lax.rem(z + 2, NZ) * 2 + c
    mate = z * 2 + (1 - c)
    return g, d, c, up, down, far, mate


def greet(n_group):
    g, d, c, up, down, far, mate = where_am_i()
    barrier = pltpu.get_barrier_semaphore()
    for to in (up, down, far, mate):
        pl.semaphore_signal(barrier, inc=1, device_id=(g, to), device_id_type=MESH)

    @pl.loop(1, n_group)
    def _(o):
        pl.semaphore_signal(barrier, inc=1, device_id=(lax.rem(g + o, n_group), d), device_id_type=MESH)

    return lambda: pl.semaphore_wait(barrier, n_group + 3)


def kernel(
    seats,
    drow_ref, q_ref, p_ref, oq_ref, op_ref, top_ref,
    dest, xp, xq, place, unplace, pay_p, pay_q, marks_out, own_top, tops, plane_top, plane_tops,
    p_all, q_rows, marks, valid, scores, scores_in, soft, soft_t, dq, t1, t2, t3, ra, rb, rl, rr, dp,
    back_q, back_p, out_q, out_p,
    swap_s, swap_r, local_s, top_s, top_r, plane_s, plane_r,
    place_s, place_r, mark_s, mark_r, ring_s, ring_r, core_s, core_r,
    sum_s, sum_r, back_s, back_r, keep_s, out_s, out_r,
):
    n_group = p_all.shape[2]
    npairs, width_d = oq_ref.shape
    half_d = width_d // 2
    width = p_all.shape[4]
    rows = n_group * SEATS
    half_g = n_group // 2
    half = rows // 2
    g, d, c, up, down, far, mate = where_am_i()
    taken = pl.ds(0, seats)

    first = pl.ds(pl.multiple_of(c * half_d, width), width)
    others = pl.ds(pl.multiple_of(c * half_d + width, width), half_d - width)
    mine = pl.ds(pl.multiple_of(c * half_d, half_d), half_d)
    mate_first = pl.ds(pl.multiple_of((1 - c) * half_d, width), width)
    mate_others = pl.ds(pl.multiple_of((1 - c) * half_d + width, width), half_d - width)
    theirs = pl.ds(pl.multiple_of((1 - c) * half_d, half_d), half_d)
    head, tail = pl.ds(0, width), pl.ds(width, half_d - width)
    own_copies = [
        pltpu.make_async_copy(drow_ref, dest.at[c], local_s.at[0]),
        pltpu.make_async_copy(p_ref.at[:, first], xp.at[c, :, head], local_s.at[1]),
        pltpu.make_async_copy(p_ref.at[:, others], xp.at[c, :, tail], local_s.at[2]),
        pltpu.make_async_copy(q_ref.at[:, mine], xq.at[c], local_s.at[3]),
    ]
    swaps = [
        remote(drow_ref, dest.at[c], swap_s.at[0], swap_r.at[0], (g, mate)),
        remote(p_ref.at[:, mate_first], xp.at[c, :, head], swap_s.at[1], swap_r.at[1], (g, mate)),
        remote(p_ref.at[:, mate_others], xp.at[c, :, tail], swap_s.at[2], swap_r.at[2], (g, mate)),
        remote(q_ref.at[:, theirs], xq.at[c], swap_s.at[3], swap_r.at[3], (g, mate)),
    ]
    ready = greet(n_group)
    for copy in own_copies:
        copy.start()
    if seats < SEATS:
        rest = slice(seats, SEATS)
        empty = jnp.zeros((n_group, SEATS - seats, width), BF16)

        @pl.loop(0, CHUNKS)
        def _(k):
            for j in range(NZ):
                p_all[k, j, :, rest, :] = empty
            for ref in (q_rows, back_q, back_p):
                ref[k, :, rest, :] = empty

    ready()

    def send_all(src, dst, s, r):
        @pl.loop(1, n_group)
        def _(o):
            to = lax.rem(g + o, n_group)
            remote(src.at[to, taken], dst.at[g, taken], s, r, (to, d)).start()

    def wait_all(ref, sem):
        wait_bytes(ref.at[pl.ds(0, n_group - 1), taken], sem)

    for copy in swaps:
        copy.start()

    def arrived(i):
        own_copies[i].wait()
        swaps[i].wait_recv()

    arrived(0)
    n2 = 2 * npairs
    group = jnp.concatenate([dest[0, 0:1, :], dest[1, 0:1, :]], axis=1)
    group = lax.shift_right_logical(group, jnp.full_like(group, 3))
    along = jnp.broadcast_to(group.astype(F32), (n2, n2))
    across = along.T
    i0 = lax.broadcasted_iota(jnp.int32, (n2, n2), 0)
    i1 = lax.broadcasted_iota(jnp.int32, (n2, n2), 1)
    same = along == across
    rank_row = jnp.sum(jnp.where(same & (i0 < i1), 1.0, 0.0), axis=0, keepdims=True)
    slot_row = (group.astype(F32) * SEATS + rank_row).astype(jnp.int32)
    place[...] = jnp.where(
        lax.broadcasted_iota(jnp.int32, (rows, n2), 0) == slot_row, 1.0, 0.0
    ).astype(BF16)

    def fill(k, x, pay, into, which):
        cols = pl.ds(k * width if isinstance(k, int) else pl.multiple_of(k * width, width), width)
        part = jnp.dot(place[...], x[:, :, cols].reshape(n2, width), preferred_element_type=F32)
        pay[k] = part.astype(BF16).reshape(n_group, SEATS, width)
        send_all(pay.at[k], into, place_s.at[which, k], place_r.at[which, k])
        into[g, 0:seats] = pay[k, g, 0:seats]

    arrived(1)
    fill(0, xp, pay_p, p_all.at[0, 0], 0)

    count = jnp.sum(
        jnp.where(lax.broadcasted_iota(jnp.int32, (n_group, n2), 0) == group, 1.0, 0.0), axis=1, keepdims=True
    )
    lane = lax.broadcasted_iota(jnp.int32, (n_group, 128), 1) - lax.rem(g, 4) * SEATS
    flags = jnp.where((lane >= 0) & (lane < count.astype(jnp.int32)), 1.0, 0.0)
    for i in range(n_group):
        marks_out[i] = jnp.broadcast_to(flags[i : i + 1], (8, 128))
    marks[0, g] = marks_out[g]
    own_top[...] = jnp.broadcast_to(jnp.max(count, axis=0, keepdims=True), (8, 128))
    tops[g] = own_top[...]

    @pl.loop(1, n_group)
    def _(o):
        to = lax.rem(g + o, n_group)
        remote(marks_out.at[to], marks.at[0, g], mark_s.at[0], mark_r.at[0], (to, d)).start()
        remote(own_top, tops.at[g], top_s, top_r, (to, d)).start()

    arrived(2)

    @pl.loop(1, CHUNKS)
    def _(k):
        fill(k, xp, pay_p, p_all.at[k, 0], 0)

    arrived(3)

    @pl.loop(0, CHUNKS)
    def _(k):
        fill(k, xq, pay_q, q_rows.at[k], 1)

    rank_col = jnp.sum(jnp.where(same & (i1 < i0), 1.0, 0.0), axis=1, keepdims=True)
    slot_col = (across[:, 0:1] * SEATS + rank_col).astype(jnp.int32)
    unplace[...] = jnp.where(
        lax.broadcasted_iota(jnp.int32, (n2, rows), 1) == slot_col, 1.0, 0.0
    ).astype(BF16)

    lo, hi = pl.ds(0, half_g), pl.ds(half_g, half_g)

    def ring(k, i):
        own, above, beyond, below = (p_all.at[k, j] for j in range(4))
        src, dst, part, to = (
            (own, below, lo, up),
            (own, below, hi, up),
            (own, above, hi, down),
            (own, above, lo, down),
            (below, beyond, lo, up),
            (above, beyond, hi, down),
        )[i]
        return remote(src.at[part, taken], dst.at[part, taken], ring_s.at[k, i], ring_r.at[k, i], (g, to))

    def score_part(k, j):
        return lax.dot_general(
            q_rows[k].reshape(rows, width), p_all[k, j].reshape(rows, width),
            (((1,), (1,)), ((), ())), preferred_element_type=F32,
        )

    def start_ring(k):
        wait_all(p_all.at[k, 0], place_r.at[0, k])
        for i in (0, 2, 1, 3):
            ring(k, i).start()

    def pass_on(k):
        ring(k, 0).wait_recv()
        ring(k, 4).start()
        ring(k, 2).wait_recv()
        ring(k, 5).start()

    def add_scores(k):
        wait_all(q_rows.at[k], place_r.at[1, k])
        for i in (1, 3, 4, 5):
            ring(k, i).wait_recv()

        @pl.loop(0, NZ)
        def _(j):
            scores[j] = scores[j] + score_part(k, j)

    mark_ring = [
        remote(marks.at[0], marks.at[3], mark_s.at[1], mark_r.at[1], (g, up)),
        remote(marks.at[0], marks.at[1], mark_s.at[2], mark_r.at[2], (g, down)),
        remote(marks.at[0], marks.at[2], mark_s.at[3], mark_r.at[3], (g, far)),
    ]

    plane_copies = [
        remote(plane_top, plane_tops.at[i], plane_s.at[i], plane_r.at[i], (g, to))
        for i, to in enumerate((up, down, far))
    ]

    start_ring(0)
    wait_bytes(marks.at[0, pl.ds(0, n_group - 1)], mark_r.at[0])
    for copy in mark_ring:
        copy.start()
    start_ring(1)
    pass_on(0)
    scores[...] = jnp.zeros_like(scores)
    for copy in mark_ring:
        copy.wait_recv()
    for j in range(NZ):
        pieces = []
        for first in range(0, n_group, 4):
            flag = marks[j, first, 0:1, :]
            for i in range(first + 1, min(first + 4, n_group)):
                flag = flag + marks[j, i, 0:1, :]
            pieces.append(flag)
        flag = pieces[0] if len(pieces) == 1 else jnp.concatenate(pieces, axis=1)
        valid[j] = jnp.broadcast_to(flag[:, :rows], (8, rows))
    wait_bytes(tops.at[pl.ds(0, n_group - 1)], top_r)
    top = tops[0]
    for i in range(1, n_group):
        top = jnp.maximum(top, tops[i])
    plane_top[...] = top
    for copy in plane_copies:
        copy.start()
    soft_t[0, :, 0:128] = jnp.broadcast_to(valid[0, 0:1, :], (128, rows)).T.astype(BF16)

    @pl.loop(2, CHUNKS)
    def _(step):
        start_ring(step)
        pass_on(step - 1)
        add_scores(step - 2)

    for copy in plane_copies:
        copy.wait_recv()
    top_ref[...] = jnp.maximum(
        jnp.maximum(plane_top[...], plane_tops[0]), jnp.maximum(plane_tops[1], plane_tops[2])
    )
    pass_on(CHUNKS - 1)
    add_scores(CHUNKS - 2)

    my_rows = pl.ds(pl.multiple_of(c * half, half), half)
    mate_rows = pl.ds(pl.multiple_of((1 - c) * half, half), half)

    def share(j):
        return remote(scores.at[j, mate_rows], scores_in.at[j], core_s.at[j], core_r.at[j], (g, mate))

    last = CHUNKS - 1
    wait_all(q_rows.at[last], place_r.at[1, last])
    for j, needs in ((0, ()), (3, (1,)), (1, (3,)), (2, (4, 5))):
        for i in needs:
            ring(last, i).wait_recv()
        scores[j] = scores[j] + score_part(last, j)
        share(j).start()
    for j in range(NZ):
        share(j).wait_recv()

    tile = min(16, half)

    @pl.loop(0, half // tile)
    def _(i):
        at_out = pl.ds(pl.multiple_of(c * half + i * tile, tile), tile)
        at_in = pl.ds(pl.multiple_of(i * tile, tile), tile)
        keep = soft_t[0, at_out, 0:1].astype(F32)
        parts = []
        top = None
        for j in range(NZ):
            s = inverse_temp * (scores[j, at_out, :] + scores_in[j, at_in, :])
            s = jnp.where(valid[j, 0:1, :] > 0, s, -1e30)
            parts.append(s)
            m = jnp.max(s, axis=1, keepdims=True)
            top = m if top is None else jnp.maximum(top, m)
        total = None
        exps = []
        for s in parts:
            e = jnp.exp(s - top)
            exps.append(e)
            t = jnp.sum(e, axis=1, keepdims=True)
            total = t if total is None else total + t
        for j in range(NZ):
            soft[j, at_out, :] = (exps[j] / total * keep).astype(BF16)

    give = remote(soft.at[:, my_rows], soft.at[:, my_rows], core_s.at[NZ], core_r.at[NZ], (g, mate))
    give.start()
    my_lanes = pl.ds(pl.multiple_of(c * half, half), half)
    mate_lanes = pl.ds(pl.multiple_of((1 - c) * half, half), half)

    @pl.loop(0, NZ)
    def _(j):
        soft_t[j, :, my_lanes] = soft[j, my_rows, :].T

    give.wait_recv()

    @pl.loop(0, NZ)
    def _(j):
        soft_t[j, :, mate_lanes] = soft[j, mate_rows, :].T

    def q_of(k):
        return q_rows[k].reshape(rows, width)

    def term(k, j, first, size):
        return inverse_temp * jnp.dot(soft_t[j, pl.ds(first, size), :], q_of(k), preferred_element_type=F32)

    def blocks(x):
        return x.astype(BF16).reshape(x.shape[0] // SEATS, SEATS, width)

    def summed(k, i):
        src, dst, to = (
            (t2.at[k, lo, taken], ra.at[k, :, taken], up),
            (t2.at[k, hi, taken], rb.at[k, :, taken], down),
            (t1.at[k, hi, taken], rl.at[k, hi, taken], up),
            (t3.at[k, lo, taken], rr.at[k, lo, taken], down),
            (t1.at[k, lo, taken], rl.at[k, lo, taken], up),
            (t3.at[k, hi, taken], rr.at[k, hi, taken], down),
        )[i]
        return remote(src, dst, sum_s.at[k, i], sum_r.at[k, i], (g, to))

    def open_sums(k):
        t2[k] = blocks(term(k, 2, 0, rows))
        summed(k, 0).start()
        summed(k, 1).start()
        t1[k, hi] = blocks(term(k, 1, half, half))
        summed(k, 2).start()
        t3[k, lo] = blocks(term(k, 3, 0, half))
        summed(k, 3).start()

    def add_sums(k):
        summed(k, 0).wait_recv()
        t1[k, lo] = blocks(term(k, 1, 0, half) + ra[k].reshape(half, width).astype(F32))
        summed(k, 4).start()
        summed(k, 1).wait_recv()
        t3[k, hi] = blocks(term(k, 3, half, half) + rb[k].reshape(half, width).astype(F32))
        summed(k, 5).start()

    def query_part(k):
        acc = -p_all[k, 0].reshape(rows, width).astype(F32)
        for j in range(NZ):
            acc = acc + jnp.dot(soft[j], p_all[k, j].reshape(rows, width), preferred_element_type=F32)
        dq[k] = blocks(inverse_temp * acc)
        send_all(dq.at[k], back_q.at[k], back_s.at[0, k], back_r.at[0, k])
        back_q[k, g, 0:seats] = dq[k, g, 0:seats]

    def close_sums(k):
        own = inverse_temp * (
            jnp.dot(soft_t[0], q_of(k), preferred_element_type=F32) - q_of(k).astype(F32)
        )
        for i in (2, 3, 4, 5):
            summed(k, i).wait_recv()
        own = own + rl[k].reshape(rows, width).astype(F32) + rr[k].reshape(rows, width).astype(F32)
        dp[k] = blocks(own)
        send_all(dp.at[k], back_p.at[k], back_s.at[1, k], back_r.at[1, k])
        back_p[k, g, 0:seats] = dp[k, g, 0:seats]

    open_sums(0)
    query_part(0)
    open_sums(1)
    add_sums(0)
    query_part(1)

    @pl.loop(2, CHUNKS)
    def _(k):
        open_sums(k)
        add_sums(k - 1)
        query_part(k)
        close_sums(k - 2)

    add_sums(CHUNKS - 1)
    close_sums(CHUNKS - 2)
    close_sums(CHUNKS - 1)

    def outputs(k, which):
        out, o_ref = ((out_q, oq_ref), (out_p, op_ref))[which]
        cols = pl.ds(pl.multiple_of(c * half_d + k * width, width), width)
        return (
            pltpu.make_async_copy(out.at[k, c], o_ref.at[:, cols], keep_s.at[which, k]),
            remote(out.at[k, 1 - c], o_ref.at[:, cols], out_s.at[which, k], out_r.at[which, k], (g, mate)),
        )

    for which in range(2):
        back, out = ((back_q, out_q), (back_p, out_p))[which]

        @pl.loop(0, CHUNKS)
        def _(k):
            wait_all(back.at[k], back_r.at[which, k])
            part = jnp.dot(unplace[...], back[k].reshape(rows, width), preferred_element_type=F32)
            out[k] = part.astype(BF16).reshape(2, npairs, width)
            here, there = outputs(k, which)
            here.start()
            there.start()

    @pl.loop(0, CHUNKS)
    def _(k):
        wait_all(pay_p.at[k], place_s.at[0, k])
        wait_all(pay_q.at[k], place_s.at[1, k])
        wait_all(dq.at[k], back_s.at[0, k])
        wait_all(dp.at[k], back_s.at[1, k])
        for i in range(6):
            ring(k, i).wait_send()
            summed(k, i).wait_send()
        for which in range(2):
            here, there = outputs(k, which)
            here.wait()
            there.wait()

    wait_bytes(marks_out.at[pl.ds(0, n_group - 1)], mark_s.at[0])
    wait_bytes(tops.at[pl.ds(0, n_group - 1)], top_s)
    for copy in swaps + mark_ring + plane_copies:
        copy.wait_send()
    for j in range(NZ):
        share(j).wait_send()
    give.wait_send()


def local(queries, passages, destination):
    n_group = lax.axis_size("grp")
    npairs, width_d = queries.shape
    half_d = width_d // 2
    width = half_d // CHUNKS
    rows = n_group * SEATS
    half = rows // 2
    half_g = n_group // 2
    drow = jnp.broadcast_to(destination.reshape(1, npairs), (8, npairs))
    dma = pltpu.SemaphoreType.DMA
    in_vmem = pl.BlockSpec(memory_space=pltpu.VMEM)
    anywhere = pl.BlockSpec(memory_space=pl.ANY)

    def vm(*shape, dtype=BF16):
        return pltpu.VMEM(shape, dtype)

    tile = (8, 128)
    payload = (CHUNKS, n_group, SEATS, width)
    def call(seats, collective_id):
        scratch = [
            vm(2, 8, npairs, dtype=jnp.int32),
            vm(2, npairs, half_d), vm(2, npairs, half_d),
            vm(rows, 2 * npairs), vm(2 * npairs, rows),
            vm(*payload), vm(*payload), vm(n_group, *tile, dtype=F32),
            vm(*tile, dtype=F32), vm(n_group, *tile, dtype=F32),
            vm(*tile, dtype=F32), vm(3, *tile, dtype=F32),
            vm(CHUNKS, NZ, n_group, SEATS, width), vm(*payload),
            vm(NZ, n_group, *tile, dtype=F32), vm(NZ, 8, rows, dtype=F32),
            vm(NZ, rows, rows, dtype=F32), vm(NZ, half, rows, dtype=F32),
            vm(NZ, rows, rows), vm(NZ, rows, rows),
            vm(*payload),
            vm(*payload), vm(*payload), vm(*payload),
            vm(CHUNKS, half_g, SEATS, width), vm(CHUNKS, half_g, SEATS, width),
            vm(*payload), vm(*payload), vm(*payload),
            vm(*payload), vm(*payload),
            vm(CHUNKS, 2, npairs, width), vm(CHUNKS, 2, npairs, width),
            dma((4,)), dma((4,)), dma((4,)), dma(()), dma(()), dma((3,)), dma((3,)),
            dma((2, CHUNKS)), dma((2, CHUNKS)), dma((4,)), dma((4,)),
            dma((CHUNKS, 6)), dma((CHUNKS, 6)), dma((NZ + 1,)), dma((NZ + 1,)),
            dma((CHUNKS, 6)), dma((CHUNKS, 6)), dma((2, CHUNKS)), dma((2, CHUNKS)),
            dma((2, CHUNKS)), dma((2, CHUNKS)), dma((2, CHUNKS)),
        ]
        return pl.pallas_call(
            functools.partial(kernel, seats),
            out_shape=(
                jax.ShapeDtypeStruct((npairs, width_d), BF16),
                jax.ShapeDtypeStruct((npairs, width_d), BF16),
                jax.ShapeDtypeStruct(tile, F32),
            ),
            in_specs=[in_vmem, anywhere, anywhere],
            out_specs=(anywhere, anywhere, in_vmem),
            scratch_shapes=scratch,
            compiler_params=pltpu.CompilerParams(
                collective_id=collective_id, has_side_effects=True, vmem_limit_bytes=67043328
            ),
        )(drow, queries, passages)

    query_grads, passage_grads, top = call(FEW, 0)
    return lax.cond(
        top[0, 0] <= FEW, lambda: (query_grads, passage_grads), lambda: tuple(call(SEATS, 1)[:2])
    )


def solution(mesh):
    placed = (P(("grp", "dev"), None), P(("grp", "dev"), None), P(("grp", "dev"), None))
    return jax.shard_map(
        local,
        mesh=mesh,
        in_specs=placed,
        out_specs=(P(("grp", "dev"), None), P(("grp", "dev"), None)),
        check_vma=False,
    )
```

```python
import functools

import jax
import jax.numpy as jnp
from jax import lax
from jax.experimental import pallas as pl
from jax.experimental.pallas import tpu as pltpu
from jax.sharding import PartitionSpec as P

inverse_temp = 100.0
MESH = pl.DeviceIdType.MESH
SEATS = 32
FEW = 24
NZ = 4
CHUNKS = 8
F32, BF16 = jnp.float32, jnp.bfloat16


def wait_bytes(ref, sem):
    pltpu.make_async_copy(ref, ref, sem).wait()


def remote(src, dst, s, r, to):
    return pltpu.make_async_remote_copy(
        src_ref=src, dst_ref=dst, send_sem=s, recv_sem=r, device_id=to, device_id_type=MESH
    )


def where_am_i():
    g = lax.axis_index("grp")
    d = lax.axis_index("dev")
    c = lax.rem(d, 2)
    z = lax.div(d, 2)
    up = lax.rem(z + 1, NZ) * 2 + c
    down = lax.rem(z + NZ - 1, NZ) * 2 + c
    far = lax.rem(z + 2, NZ) * 2 + c
    mate = z * 2 + (1 - c)
    return g, d, c, up, down, far, mate


def greet(n_group):
    g, d, c, up, down, far, mate = where_am_i()
    barrier = pltpu.get_barrier_semaphore()
    for to in (up, down, far, mate):
        pl.semaphore_signal(barrier, inc=1, device_id=(g, to), device_id_type=MESH)

    @pl.loop(1, n_group)
    def _(o):
        pl.semaphore_signal(barrier, inc=1, device_id=(lax.rem(g + o, n_group), d), device_id_type=MESH)

    return lambda: pl.semaphore_wait(barrier, n_group + 3)


def kernel(
    seats,
    drow_ref, q_ref, p_ref, oq_ref, op_ref, top_ref,
    dest, xp, xq, place, unplace, pay_p, pay_q, marks_out, own_top, tops, plane_top, plane_tops,
    p_all, q_rows, marks, valid, scores, scores_in, soft, soft_t, dq, t1, t2, t3, ra, rb, rl, rr, dp,
    back_q, back_p, out_q, out_p,
    swap_s, swap_r, local_s, top_s, top_r, plane_s, plane_r,
    place_s, place_r, mark_s, mark_r, ring_s, ring_r, core_s, core_r, give_s, give_r,
    sum_s, sum_r, back_s, back_r, keep_s, out_s, out_r,
):
    n_group = p_all.shape[2]
    npairs, width_d = oq_ref.shape
    half_d = width_d // 2
    width = p_all.shape[4]
    rows = n_group * SEATS
    half_g = n_group // 2
    half = rows // 2
    g, d, c, up, down, far, mate = where_am_i()
    taken = pl.ds(0, seats)

    first = pl.ds(pl.multiple_of(c * half_d, width), width)
    others = pl.ds(pl.multiple_of(c * half_d + width, width), half_d - width)
    mine = pl.ds(pl.multiple_of(c * half_d, half_d), half_d)
    mate_first = pl.ds(pl.multiple_of((1 - c) * half_d, width), width)
    mate_others = pl.ds(pl.multiple_of((1 - c) * half_d + width, width), half_d - width)
    theirs = pl.ds(pl.multiple_of((1 - c) * half_d, half_d), half_d)
    head, tail = pl.ds(0, width), pl.ds(width, half_d - width)
    own_copies = [
        pltpu.make_async_copy(drow_ref, dest.at[c], local_s.at[0]),
        pltpu.make_async_copy(p_ref.at[:, first], xp.at[c, :, head], local_s.at[1]),
        pltpu.make_async_copy(p_ref.at[:, others], xp.at[c, :, tail], local_s.at[2]),
        pltpu.make_async_copy(q_ref.at[:, mine], xq.at[c], local_s.at[3]),
    ]
    swaps = [
        remote(drow_ref, dest.at[c], swap_s.at[0], swap_r.at[0], (g, mate)),
        remote(p_ref.at[:, mate_first], xp.at[c, :, head], swap_s.at[1], swap_r.at[1], (g, mate)),
        remote(p_ref.at[:, mate_others], xp.at[c, :, tail], swap_s.at[2], swap_r.at[2], (g, mate)),
        remote(q_ref.at[:, theirs], xq.at[c], swap_s.at[3], swap_r.at[3], (g, mate)),
    ]
    ready = greet(n_group)
    for copy in own_copies:
        copy.start()
    if seats < SEATS:
        rest = slice(seats, SEATS)
        empty = jnp.zeros((n_group, SEATS - seats, width), BF16)

        @pl.loop(0, CHUNKS)
        def _(k):
            for j in range(NZ):
                p_all[k, j, :, rest, :] = empty
            for ref in (q_rows, back_q, back_p):
                ref[k, :, rest, :] = empty

    ready()

    def send_all(src, dst, s, r):
        @pl.loop(1, n_group)
        def _(o):
            to = lax.rem(g + o, n_group)
            remote(src.at[to, taken], dst.at[g, taken], s, r, (to, d)).start()

    def wait_all(ref, sem):
        wait_bytes(ref.at[pl.ds(0, n_group - 1), taken], sem)

    for copy in swaps:
        copy.start()

    def arrived(i):
        own_copies[i].wait()
        swaps[i].wait_recv()

    arrived(0)
    n2 = 2 * npairs
    group = jnp.concatenate([dest[0, 0:1, :], dest[1, 0:1, :]], axis=1)
    group = lax.shift_right_logical(group, jnp.full_like(group, 3))
    along = jnp.broadcast_to(group.astype(F32), (n2, n2))
    across = along.T
    i0 = lax.broadcasted_iota(jnp.int32, (n2, n2), 0)
    i1 = lax.broadcasted_iota(jnp.int32, (n2, n2), 1)
    same = along == across
    rank_row = jnp.sum(jnp.where(same & (i0 < i1), 1.0, 0.0), axis=0, keepdims=True)
    slot_row = (group.astype(F32) * SEATS + rank_row).astype(jnp.int32)
    place[...] = jnp.where(
        lax.broadcasted_iota(jnp.int32, (rows, n2), 0) == slot_row, 1.0, 0.0
    ).astype(BF16)

    def fill(k, x, pay, into, which):
        cols = pl.ds(k * width if isinstance(k, int) else pl.multiple_of(k * width, width), width)
        part = jnp.dot(place[...], x[:, :, cols].reshape(n2, width), preferred_element_type=F32)
        pay[k] = part.astype(BF16).reshape(n_group, SEATS, width)
        send_all(pay.at[k], into, place_s.at[which, k], place_r.at[which, k])
        into[g, 0:seats] = pay[k, g, 0:seats]

    arrived(1)
    fill(0, xp, pay_p, p_all.at[0, 0], 0)

    count = jnp.sum(
        jnp.where(lax.broadcasted_iota(jnp.int32, (n_group, n2), 0) == group, 1.0, 0.0), axis=1, keepdims=True
    )
    lane = lax.broadcasted_iota(jnp.int32, (n_group, 128), 1) - lax.rem(g, 4) * SEATS
    flags = jnp.where((lane >= 0) & (lane < count.astype(jnp.int32)), 1.0, 0.0)
    for i in range(n_group):
        marks_out[i] = jnp.broadcast_to(flags[i : i + 1], (8, 128))
    marks[0, g] = marks_out[g]
    own_top[...] = jnp.broadcast_to(jnp.max(count, axis=0, keepdims=True), (8, 128))
    tops[g] = own_top[...]

    @pl.loop(1, n_group)
    def _(o):
        to = lax.rem(g + o, n_group)
        remote(marks_out.at[to], marks.at[0, g], mark_s.at[0], mark_r.at[0], (to, d)).start()
        remote(own_top, tops.at[g], top_s, top_r, (to, d)).start()

    arrived(2)

    def fill_p(k):
        fill(k, xp, pay_p, p_all.at[k, 0], 0)

    def fill_q(k):
        fill(k, xq, pay_q, q_rows.at[k], 1)

    fill_p(1)

    lo, hi = pl.ds(0, half_g), pl.ds(half_g, half_g)

    def ring(k, i):
        own, above, beyond, below = (p_all.at[k, j] for j in range(4))
        src, dst, part, to = (
            (own, below, lo, up),
            (own, below, hi, up),
            (own, above, hi, down),
            (own, above, lo, down),
            (below, beyond, lo, up),
            (above, beyond, hi, down),
        )[i]
        return remote(src.at[part, taken], dst.at[part, taken], ring_s.at[k, i], ring_r.at[k, i], (g, to))

    def score_part(k, j):
        return lax.dot_general(
            q_rows[k].reshape(rows, width), p_all[k, j].reshape(rows, width),
            (((1,), (1,)), ((), ())), preferred_element_type=F32,
        ).reshape(n_group, SEATS, rows)

    def start_ring(k):
        wait_all(p_all.at[k, 0], place_r.at[0, k])
        for i in (0, 2, 1, 3):
            ring(k, i).start()

    def pass_on(k):
        ring(k, 0).wait_recv()
        ring(k, 4).start()
        ring(k, 2).wait_recv()
        ring(k, 5).start()

    def add_scores(k):
        wait_all(q_rows.at[k], place_r.at[1, k])
        for i in (1, 3, 4, 5):
            ring(k, i).wait_recv()

        @pl.loop(0, NZ)
        def _(j):
            scores[j] = scores[j] + score_part(k, j)

    mark_ring = [
        remote(marks.at[0], marks.at[3], mark_s.at[1], mark_r.at[1], (g, up)),
        remote(marks.at[0], marks.at[1], mark_s.at[2], mark_r.at[2], (g, down)),
        remote(marks.at[0], marks.at[2], mark_s.at[3], mark_r.at[3], (g, far)),
    ]

    plane_copies = [
        remote(plane_top, plane_tops.at[i], plane_s.at[i], plane_r.at[i], (g, to))
        for i, to in enumerate((up, down, far))
    ]

    start_ring(0)
    fill_p(2)
    arrived(3)
    fill_q(0)
    wait_bytes(marks.at[0, pl.ds(0, n_group - 1)], mark_r.at[0])
    for copy in mark_ring:
        copy.start()
    start_ring(1)
    pass_on(0)
    fill_p(3)
    fill_q(1)
    scores[...] = jnp.zeros_like(scores)
    soft[...] = jnp.zeros_like(soft)
    rank_col = jnp.sum(jnp.where(same & (i1 < i0), 1.0, 0.0), axis=1, keepdims=True)
    slot_col = (across[:, 0:1] * SEATS + rank_col).astype(jnp.int32)
    unplace[...] = jnp.where(
        lax.broadcasted_iota(jnp.int32, (n2, rows), 1) == slot_col, 1.0, 0.0
    ).astype(BF16)
    for copy in mark_ring:
        copy.wait_recv()
    for j in range(NZ):
        pieces = []
        for first in range(0, n_group, 4):
            flag = marks[j, first, 0:1, :]
            for i in range(first + 1, min(first + 4, n_group)):
                flag = flag + marks[j, i, 0:1, :]
            pieces.append(flag)
        flag = pieces[0] if len(pieces) == 1 else jnp.concatenate(pieces, axis=1)
        valid[j] = jnp.broadcast_to(flag[:, :rows], (8, rows))
    wait_bytes(tops.at[pl.ds(0, n_group - 1)], top_r)
    top = tops[0]
    for i in range(1, n_group):
        top = jnp.maximum(top, tops[i])
    plane_top[...] = top
    for copy in plane_copies:
        copy.start()
    soft_t[0, :, 0:128] = jnp.broadcast_to(valid[0, 0:1, :], (128, rows)).T.astype(BF16)

    @pl.loop(2, CHUNKS - 2)
    def _(step):
        start_ring(step)
        pass_on(step - 1)
        fill_p(step + 2)
        fill_q(step)
        add_scores(step - 2)

    @pl.loop(CHUNKS - 2, CHUNKS)
    def _(step):
        start_ring(step)
        pass_on(step - 1)
        fill_q(step)
        add_scores(step - 2)

    for copy in plane_copies:
        copy.wait_recv()
    top_ref[...] = jnp.maximum(
        jnp.maximum(plane_top[...], plane_tops[0]), jnp.maximum(plane_tops[1], plane_tops[2])
    )
    pass_on(CHUNKS - 1)
    add_scores(CHUNKS - 2)

    mate_seats = pl.ds((1 - c) * half_g, half_g)

    def share(j):
        return remote(scores.at[j, mate_seats, taken], scores_in.at[j, :, taken], core_s.at[j], core_r.at[j], (g, mate))

    last = CHUNKS - 1
    wait_all(q_rows.at[last], place_r.at[1, last])
    for j, needs in ((0, ()), (3, (1,)), (1, (3,)), (2, (4, 5))):
        for i in needs:
            ring(last, i).wait_recv()
        scores[j] = scores[j] + score_part(last, j)
        share(j).start()
    for j in range(NZ):
        share(j).wait_recv()

    def softmax_of(i):
        n = c * half_g + i
        keep = soft_t[0, pl.ds(pl.multiple_of(n * SEATS, SEATS), SEATS), 0:1].astype(F32)
        parts = []
        top = None
        for j in range(NZ):
            s = inverse_temp * (scores[j, n] + scores_in[j, i])
            s = jnp.where(valid[j, 0:1, :] > 0, s, -1e30)
            parts.append(s)
            m = jnp.max(s, axis=1, keepdims=True)
            top = m if top is None else jnp.maximum(top, m)
        total = None
        exps = []
        for s in parts:
            e = jnp.exp(s - top)
            exps.append(e)
            t = jnp.sum(e, axis=1, keepdims=True)
            total = t if total is None else total + t
        for j in range(NZ):
            soft[j, n] = jnp.where(keep > 0, exps[j] / total, 0.0).astype(BF16)

    pieces = min(4, half_g)
    piece = half_g // pieces

    def give(i):
        part = pl.ds(c * half_g + i * piece, piece)
        return remote(soft.at[:, part, taken], soft.at[:, part, taken], give_s.at[i], give_r.at[i], (g, mate))

    for i in range(pieces):

        @pl.loop(i * piece, (i + 1) * piece, unroll=True)
        def _(n):
            softmax_of(n)

        give(i).start()
    my_lanes = pl.ds(pl.multiple_of(c * half, half), half)
    mate_lanes = pl.ds(pl.multiple_of((1 - c) * half, half), half)
    my_seats = pl.ds(c * half_g, half_g)

    @pl.loop(0, NZ)
    def _(j):
        soft_t[j, :, my_lanes] = soft[j, my_seats].reshape(half, rows).T

    for i in range(pieces):
        give(i).wait_recv()

    @pl.loop(0, NZ)
    def _(j):
        soft_t[j, :, mate_lanes] = soft[j, mate_seats].reshape(half, rows).T

    def q_of(k):
        return q_rows[k].reshape(rows, width)

    def term(k, j, first, size):
        return inverse_temp * jnp.dot(soft_t[j, pl.ds(first, size), :], q_of(k), preferred_element_type=F32)

    def blocks(x):
        return x.astype(BF16).reshape(x.shape[0] // SEATS, SEATS, width)

    def summed(k, i):
        src, dst, to = (
            (t2.at[k, lo, taken], ra.at[k, :, taken], up),
            (t2.at[k, hi, taken], rb.at[k, :, taken], down),
            (t1.at[k, hi, taken], rl.at[k, hi, taken], up),
            (t3.at[k, lo, taken], rr.at[k, lo, taken], down),
            (t1.at[k, lo, taken], rl.at[k, lo, taken], up),
            (t3.at[k, hi, taken], rr.at[k, hi, taken], down),
        )[i]
        return remote(src, dst, sum_s.at[k, i], sum_r.at[k, i], (g, to))

    def open_sums(k):
        t2[k] = blocks(term(k, 2, 0, rows))
        summed(k, 0).start()
        summed(k, 1).start()
        t1[k, hi] = blocks(term(k, 1, half, half))
        summed(k, 2).start()
        t3[k, lo] = blocks(term(k, 3, 0, half))
        summed(k, 3).start()

    def add_sums(k):
        summed(k, 0).wait_recv()
        t1[k, lo] = blocks(term(k, 1, 0, half) + ra[k].reshape(half, width).astype(F32))
        summed(k, 4).start()
        summed(k, 1).wait_recv()
        t3[k, hi] = blocks(term(k, 3, half, half) + rb[k].reshape(half, width).astype(F32))
        summed(k, 5).start()

    def query_part(k):
        acc = -p_all[k, 0].reshape(rows, width).astype(F32)
        for j in range(NZ):
            acc = acc + jnp.dot(soft[j].reshape(rows, rows), p_all[k, j].reshape(rows, width), preferred_element_type=F32)
        dq[k] = blocks(inverse_temp * acc)
        send_all(dq.at[k], back_q.at[k], back_s.at[0, k], back_r.at[0, k])
        back_q[k, g, 0:seats] = dq[k, g, 0:seats]

    def close_sums(k):
        own = inverse_temp * (
            jnp.dot(soft_t[0], q_of(k), preferred_element_type=F32) - q_of(k).astype(F32)
        )
        for i in (2, 3, 4, 5):
            summed(k, i).wait_recv()
        own = own + rl[k].reshape(rows, width).astype(F32) + rr[k].reshape(rows, width).astype(F32)
        dp[k] = blocks(own)
        send_all(dp.at[k], back_p.at[k], back_s.at[1, k], back_r.at[1, k])
        back_p[k, g, 0:seats] = dp[k, g, 0:seats]

    open_sums(0)
    query_part(0)
    open_sums(1)
    add_sums(0)
    query_part(1)

    @pl.loop(2, CHUNKS)
    def _(k):
        open_sums(k)
        add_sums(k - 1)
        query_part(k)
        close_sums(k - 2)

    add_sums(CHUNKS - 1)
    close_sums(CHUNKS - 2)
    close_sums(CHUNKS - 1)

    def outputs(k, which):
        out, o_ref = ((out_q, oq_ref), (out_p, op_ref))[which]
        cols = pl.ds(pl.multiple_of(c * half_d + k * width, width), width)
        return (
            pltpu.make_async_copy(out.at[k, c], o_ref.at[:, cols], keep_s.at[which, k]),
            remote(out.at[k, 1 - c], o_ref.at[:, cols], out_s.at[which, k], out_r.at[which, k], (g, mate)),
        )

    for which in range(2):
        back, out = ((back_q, out_q), (back_p, out_p))[which]

        @pl.loop(0, CHUNKS)
        def _(k):
            wait_all(back.at[k], back_r.at[which, k])
            part = jnp.dot(unplace[...], back[k].reshape(rows, width), preferred_element_type=F32)
            out[k] = part.astype(BF16).reshape(2, npairs, width)
            here, there = outputs(k, which)
            here.start()
            there.start()

    @pl.loop(0, CHUNKS)
    def _(k):
        wait_all(pay_p.at[k], place_s.at[0, k])
        wait_all(pay_q.at[k], place_s.at[1, k])
        wait_all(dq.at[k], back_s.at[0, k])
        wait_all(dp.at[k], back_s.at[1, k])
        for i in range(6):
            ring(k, i).wait_send()
            summed(k, i).wait_send()
        for which in range(2):
            here, there = outputs(k, which)
            here.wait()
            there.wait()

    wait_bytes(marks_out.at[pl.ds(0, n_group - 1)], mark_s.at[0])
    wait_bytes(tops.at[pl.ds(0, n_group - 1)], top_s)
    for copy in swaps + mark_ring + plane_copies:
        copy.wait_send()
    for j in range(NZ):
        share(j).wait_send()
    for i in range(pieces):
        give(i).wait_send()


def local(queries, passages, destination):
    n_group = lax.axis_size("grp")
    npairs, width_d = queries.shape
    half_d = width_d // 2
    width = half_d // CHUNKS
    rows = n_group * SEATS
    half = rows // 2
    half_g = n_group // 2
    drow = jnp.broadcast_to(destination.reshape(1, npairs), (8, npairs))
    dma = pltpu.SemaphoreType.DMA
    in_vmem = pl.BlockSpec(memory_space=pltpu.VMEM)
    anywhere = pl.BlockSpec(memory_space=pl.ANY)

    def vm(*shape, dtype=BF16):
        return pltpu.VMEM(shape, dtype)

    tile = (8, 128)
    payload = (CHUNKS, n_group, SEATS, width)
    def call(seats, collective_id):
        scratch = [
            vm(2, 8, npairs, dtype=jnp.int32),
            vm(2, npairs, half_d), vm(2, npairs, half_d),
            vm(rows, 2 * npairs), vm(2 * npairs, rows),
            vm(*payload), vm(*payload), vm(n_group, *tile, dtype=F32),
            vm(*tile, dtype=F32), vm(n_group, *tile, dtype=F32),
            vm(*tile, dtype=F32), vm(3, *tile, dtype=F32),
            vm(CHUNKS, NZ, n_group, SEATS, width), vm(*payload),
            vm(NZ, n_group, *tile, dtype=F32), vm(NZ, 8, rows, dtype=F32),
            vm(NZ, n_group, SEATS, rows, dtype=F32), vm(NZ, half_g, SEATS, rows, dtype=F32),
            vm(NZ, n_group, SEATS, rows), vm(NZ, rows, rows),
            vm(*payload),
            vm(*payload), vm(*payload), vm(*payload),
            vm(CHUNKS, half_g, SEATS, width), vm(CHUNKS, half_g, SEATS, width),
            vm(*payload), vm(*payload), vm(*payload),
            vm(*payload), vm(*payload),
            vm(CHUNKS, 2, npairs, width), vm(CHUNKS, 2, npairs, width),
            dma((4,)), dma((4,)), dma((4,)), dma(()), dma(()), dma((3,)), dma((3,)),
            dma((2, CHUNKS)), dma((2, CHUNKS)), dma((4,)), dma((4,)),
            dma((CHUNKS, 6)), dma((CHUNKS, 6)), dma((NZ,)), dma((NZ,)), dma((4,)), dma((4,)),
            dma((CHUNKS, 6)), dma((CHUNKS, 6)), dma((2, CHUNKS)), dma((2, CHUNKS)),
            dma((2, CHUNKS)), dma((2, CHUNKS)), dma((2, CHUNKS)),
        ]
        return pl.pallas_call(
            functools.partial(kernel, seats),
            out_shape=(
                jax.ShapeDtypeStruct((npairs, width_d), BF16),
                jax.ShapeDtypeStruct((npairs, width_d), BF16),
                jax.ShapeDtypeStruct(tile, F32),
            ),
            in_specs=[in_vmem, anywhere, anywhere],
            out_specs=(anywhere, anywhere, in_vmem),
            scratch_shapes=scratch,
            compiler_params=pltpu.CompilerParams(
                collective_id=collective_id, has_side_effects=True, vmem_limit_bytes=67043328
            ),
        )(drow, queries, passages)

    query_grads, passage_grads, top = call(FEW, 0)
    return lax.cond(
        top[0, 0] <= FEW, lambda: (query_grads, passage_grads), lambda: tuple(call(SEATS, 1)[:2])
    )


def solution(mesh):
    placed = (P(("grp", "dev"), None), P(("grp", "dev"), None), P(("grp", "dev"), None))
    return jax.shard_map(
        local,
        mesh=mesh,
        in_specs=placed,
        out_specs=(P(("grp", "dev"), None), P(("grp", "dev"), None)),
        check_vma=False,
    )
```

```python
import functools

import jax
import jax.numpy as jnp
from jax import lax
from jax.experimental import pallas as pl
from jax.experimental.pallas import tpu as pltpu
from jax.sharding import PartitionSpec as P

inverse_temp = 100.0
MESH = pl.DeviceIdType.MESH
SEATS = 32
FEW = 24
NZ = 4
CHUNKS = 8
RAW = 2
F32, BF16 = jnp.float32, jnp.bfloat16


def wait_bytes(ref, sem):
    pltpu.make_async_copy(ref, ref, sem).wait()


def remote(src, dst, s, r, to):
    return pltpu.make_async_remote_copy(
        src_ref=src, dst_ref=dst, send_sem=s, recv_sem=r, device_id=to, device_id_type=MESH
    )


def where_am_i():
    g = lax.axis_index("grp")
    d = lax.axis_index("dev")
    c = lax.rem(d, 2)
    z = lax.div(d, 2)
    up = lax.rem(z + 1, NZ) * 2 + c
    down = lax.rem(z + NZ - 1, NZ) * 2 + c
    far = lax.rem(z + 2, NZ) * 2 + c
    mate = z * 2 + (1 - c)
    return g, d, c, up, down, far, mate


def greet(n_group):
    g, d, c, up, down, far, mate = where_am_i()
    barrier = pltpu.get_barrier_semaphore()
    for to in (up, down, far, mate):
        pl.semaphore_signal(barrier, inc=1, device_id=(g, to), device_id_type=MESH)

    @pl.loop(1, n_group)
    def _(o):
        pl.semaphore_signal(barrier, inc=1, device_id=(lax.rem(g + o, n_group), d), device_id_type=MESH)

    return lambda: pl.semaphore_wait(barrier, n_group + 3)


def kernel(
    seats,
    drow_ref, q_ref, p_ref, oq_ref, op_ref, top_ref,
    dest, raw_x, raw_pay, xp, xq, place, unplace, pay_p, pay_q, marks_out, own_top, tops, plane_top, plane_tops,
    p_all, q_rows, marks, valid, scores, scores_in, soft, soft_t, dq, t1, t2, t3, ra, rb, rl, rr, dp,
    back_q, back_p, out_q, out_p,
    swap_s, swap_r, local_s, dest_s, dest_r, raw_s, raw_r, top_s, top_r, plane_s, plane_r,
    place_s, place_r, mark_s, mark_r, ring_s, ring_r, core_s, core_r, give_s, give_r,
    sum_s, sum_r, back_s, back_r, keep_s, out_s, out_r,
):
    n_group = p_all.shape[2]
    npairs, width_d = oq_ref.shape
    half_d = width_d // 2
    width = p_all.shape[4]
    rows = n_group * SEATS
    half_g = n_group // 2
    half = rows // 2
    g, d, c, up, down, far, mate = where_am_i()
    taken = pl.ds(0, seats)

    early = RAW * width
    first = pl.ds(pl.multiple_of(c * half_d, early), early)
    others = pl.ds(pl.multiple_of(c * half_d + early, early), half_d - early)
    mine = pl.ds(pl.multiple_of(c * half_d, half_d), half_d)
    mate_first = pl.ds(pl.multiple_of((1 - c) * half_d, early), early)
    mate_others = pl.ds(pl.multiple_of((1 - c) * half_d + early, early), half_d - early)
    theirs = pl.ds(pl.multiple_of((1 - c) * half_d, half_d), half_d)
    tail = pl.ds(early, half_d - early)
    own_copies = [
        pltpu.make_async_copy(drow_ref, dest.at[0, c], local_s.at[0]),
        pltpu.make_async_copy(p_ref.at[:, first], raw_x.at[0, c], local_s.at[1]),
        pltpu.make_async_copy(p_ref.at[:, others], xp.at[c, :, tail], local_s.at[2]),
        pltpu.make_async_copy(q_ref.at[:, mine], xq.at[c], local_s.at[3]),
    ]
    swaps = [
        remote(drow_ref, dest.at[0, c], swap_s.at[0], swap_r.at[0], (g, mate)),
        remote(p_ref.at[:, mate_first], raw_x.at[0, c], swap_s.at[1], swap_r.at[1], (g, mate)),
        remote(p_ref.at[:, mate_others], xp.at[c, :, tail], swap_s.at[2], swap_r.at[2], (g, mate)),
        remote(q_ref.at[:, theirs], xq.at[c], swap_s.at[3], swap_r.at[3], (g, mate)),
    ]
    ready = greet(n_group)
    for copy in own_copies:
        copy.start()
    if seats < SEATS:
        rest = slice(seats, SEATS)
        empty = jnp.zeros((n_group, SEATS - seats, width), BF16)

        @pl.loop(0, CHUNKS)
        def _(k):
            for j in range(NZ):
                p_all[k, j, :, rest, :] = empty
            for ref in (q_rows, back_q, back_p):
                ref[k, :, rest, :] = empty

    ready()

    def send_all(src, dst, s, r):
        @pl.loop(1, n_group)
        def _(o):
            to = lax.rem(g + o, n_group)
            remote(src.at[to, taken], dst.at[g, taken], s, r, (to, d)).start()

    def wait_all(ref, sem):
        wait_bytes(ref.at[pl.ds(0, n_group - 1), taken], sem)

    for copy in swaps:
        copy.start()

    def arrived(i):
        own_copies[i].wait()
        swaps[i].wait_recv()

    n2 = 2 * npairs
    i0 = lax.broadcasted_iota(jnp.int32, (n2, n2), 0)
    i1 = lax.broadcasted_iota(jnp.int32, (n2, n2), 1)

    def groups_of(j):
        group = jnp.concatenate([dest[j, 0, 0:1, :], dest[j, 1, 0:1, :]], axis=1)
        group = lax.shift_right_logical(group, jnp.full_like(group, 3))
        across = jnp.broadcast_to(group.astype(F32), (n2, n2)).T
        return group, across, group.astype(F32) == across

    def placing(group, same):
        rank_row = jnp.sum(jnp.where(same & (i0 < i1), 1.0, 0.0), axis=0, keepdims=True)
        slot_row = (group.astype(F32) * SEATS + rank_row).astype(jnp.int32)
        return jnp.where(lax.broadcasted_iota(jnp.int32, (rows, n2), 0) == slot_row, 1.0, 0.0).astype(BF16)

    dest_copies = [
        remote(dest.at[0], dest.at[j], dest_s.at[j - 1], dest_r.at[j - 1], (g, to))
        for j, to in ((1, down), (2, far), (3, up))
    ]

    def raw(i):
        src, dst, core, to = (
            (0, 3, 0, up), (0, 3, 1, up), (0, 1, 1, down), (0, 1, 0, down), (3, 2, 0, up), (1, 2, 1, down)
        )[i]
        return remote(raw_x.at[src, core], raw_x.at[dst, core], ring_s.at[0, i], ring_r.at[0, i], (g, to))

    arrived(0)
    arrived(1)
    for i in (0, 2, 1, 3):
        raw(i).start()
    for copy in dest_copies:
        copy.start()
    group, across, same = groups_of(0)
    place[...] = placing(group, same)

    def fill_from(placer, x, pay, into, s, r):
        part = jnp.dot(placer, x.reshape(n2, width), preferred_element_type=F32)
        pay[...] = part.astype(BF16).reshape(n_group, SEATS, width)
        send_all(pay, into, s, r)
        into[g, 0:seats] = pay[g, 0:seats]

    def columns(k):
        return pl.ds(k * width if isinstance(k, int) else pl.multiple_of(k * width, width), width)

    def fill_p(k):
        fill_from(
            place[...], xp[:, :, columns(k)], pay_p.at[k], p_all.at[k, 0], place_s.at[0, k], place_r.at[0, k]
        )

    def fill_q(k):
        fill_from(place[...], xq[:, :, columns(k)], pay_q.at[k], q_rows.at[k], place_s.at[1, k], place_r.at[1, k])

    def fill_own(k):
        fill_from(
            place[...], raw_x[0, :, :, columns(k)], pay_p.at[k], p_all.at[k, 0], place_s.at[0, k], place_r.at[0, k]
        )

    def fill_raw(j):
        group, _, same = groups_of(j)
        placer = placing(group, same)
        for k in range(RAW):
            fill_from(
                placer, raw_x[j, :, :, columns(k)], raw_pay.at[k, j - 1], p_all.at[k, j],
                raw_s.at[k, j - 1], raw_r.at[k, j - 1],
            )

    arrived(2)
    fill_p(2)
    raw(0).wait_recv()
    raw(4).start()
    raw(2).wait_recv()
    raw(5).start()

    @pl.loop(3, 5)
    def _(k):
        fill_p(k)

    count = jnp.sum(
        jnp.where(lax.broadcasted_iota(jnp.int32, (n_group, n2), 0) == group, 1.0, 0.0), axis=1, keepdims=True
    )
    lane = lax.broadcasted_iota(jnp.int32, (n_group, 128), 1) - lax.rem(g, 4) * SEATS
    flags = jnp.where((lane >= 0) & (lane < count.astype(jnp.int32)), 1.0, 0.0)
    for i in range(n_group):
        marks_out[i] = jnp.broadcast_to(flags[i : i + 1], (8, 128))
    marks[0, g] = marks_out[g]
    own_top[...] = jnp.broadcast_to(jnp.max(count, axis=0, keepdims=True), (8, 128))
    tops[g] = own_top[...]

    @pl.loop(1, n_group)
    def _(o):
        to = lax.rem(g + o, n_group)
        remote(marks_out.at[to], marks.at[0, g], mark_s.at[0], mark_r.at[0], (to, d)).start()
        remote(own_top, tops.at[g], top_s, top_r, (to, d)).start()

    arrived(3)
    fill_q(2)

    lo, hi = pl.ds(0, half_g), pl.ds(half_g, half_g)

    def ring(k, i):
        own, above, beyond, below = (p_all.at[k, j] for j in range(4))
        src, dst, part, to = (
            (own, below, lo, up),
            (own, below, hi, up),
            (own, above, hi, down),
            (own, above, lo, down),
            (below, beyond, lo, up),
            (above, beyond, hi, down),
        )[i]
        return remote(src.at[part, taken], dst.at[part, taken], ring_s.at[k, i], ring_r.at[k, i], (g, to))

    def score_part(k, j):
        return lax.dot_general(
            q_rows[k].reshape(rows, width), p_all[k, j].reshape(rows, width),
            (((1,), (1,)), ((), ())), preferred_element_type=F32,
        ).reshape(n_group, SEATS, rows)

    def start_ring(k):
        wait_all(p_all.at[k, 0], place_r.at[0, k])
        for i in (0, 2, 1, 3):
            ring(k, i).start()

    def pass_on(k):
        ring(k, 0).wait_recv()
        ring(k, 4).start()
        ring(k, 2).wait_recv()
        ring(k, 5).start()

    def add_scores(k):
        wait_all(q_rows.at[k], place_r.at[1, k])
        if isinstance(k, int) and k < RAW:
            wait_all(p_all.at[k, 0], place_r.at[0, k])
            for j in range(1, NZ):
                wait_all(p_all.at[k, j], raw_r.at[k, j - 1])
        else:
            for i in (1, 3, 4, 5):
                ring(k, i).wait_recv()

        @pl.loop(0, NZ)
        def _(j):
            scores[j] = scores[j] + score_part(k, j)

    mark_ring = [
        remote(marks.at[0], marks.at[3], mark_s.at[1], mark_r.at[1], (g, up)),
        remote(marks.at[0], marks.at[1], mark_s.at[2], mark_r.at[2], (g, down)),
        remote(marks.at[0], marks.at[2], mark_s.at[3], mark_r.at[3], (g, far)),
    ]

    plane_copies = [
        remote(plane_top, plane_tops.at[i], plane_s.at[i], plane_r.at[i], (g, to))
        for i, to in enumerate((up, down, far))
    ]

    start_ring(2)
    fill_p(5)
    fill_q(3)
    fill_p(6)
    wait_bytes(marks.at[0, pl.ds(0, n_group - 1)], mark_r.at[0])
    for copy in mark_ring:
        copy.start()
    scores[...] = jnp.zeros_like(scores)
    soft[...] = jnp.zeros_like(soft)
    rank_col = jnp.sum(jnp.where(same & (i1 < i0), 1.0, 0.0), axis=1, keepdims=True)
    slot_col = (across[:, 0:1] * SEATS + rank_col).astype(jnp.int32)
    unplace[...] = jnp.where(
        lax.broadcasted_iota(jnp.int32, (n2, rows), 1) == slot_col, 1.0, 0.0
    ).astype(BF16)

    start_ring(3)
    pass_on(2)
    fill_p(7)
    fill_q(4)
    for copy in mark_ring:
        copy.wait_recv()
    for j in range(NZ):
        pieces = []
        for first_mark in range(0, n_group, 4):
            flag = marks[j, first_mark, 0:1, :]
            for i in range(first_mark + 1, min(first_mark + 4, n_group)):
                flag = flag + marks[j, i, 0:1, :]
            pieces.append(flag)
        flag = pieces[0] if len(pieces) == 1 else jnp.concatenate(pieces, axis=1)
        valid[j] = jnp.broadcast_to(flag[:, :rows], (8, rows))
    wait_bytes(tops.at[pl.ds(0, n_group - 1)], top_r)
    top = tops[0]
    for i in range(1, n_group):
        top = jnp.maximum(top, tops[i])
    plane_top[...] = top
    for copy in plane_copies:
        copy.start()
    soft_t[0, :, 0:128] = jnp.broadcast_to(valid[0, 0:1, :], (128, rows)).T.astype(BF16)
    for copy in dest_copies:
        copy.wait_recv()
    for i in (1, 3, 4, 5):
        raw(i).wait_recv()

    for k in range(RAW):
        fill_own(k)

    @pl.loop(4, 7)
    def _(step):
        start_ring(step)
        pass_on(step - 1)
        fill_raw(step - 3)
        fill_q(step + 1)
        add_scores(step - 2)

    start_ring(7)
    pass_on(6)
    fill_q(0)
    fill_q(1)
    add_scores(5)
    for copy in plane_copies:
        copy.wait_recv()
    top_ref[...] = jnp.maximum(
        jnp.maximum(plane_top[...], plane_tops[0]), jnp.maximum(plane_tops[1], plane_tops[2])
    )
    pass_on(7)
    add_scores(6)
    add_scores(0)
    add_scores(1)

    mate_seats = pl.ds((1 - c) * half_g, half_g)

    def share(j):
        return remote(scores.at[j, mate_seats, taken], scores_in.at[j, :, taken], core_s.at[j], core_r.at[j], (g, mate))

    last = CHUNKS - 1
    wait_all(q_rows.at[last], place_r.at[1, last])
    for j, needs in ((0, ()), (3, (1,)), (1, (3,)), (2, (4, 5))):
        for i in needs:
            ring(last, i).wait_recv()
        scores[j] = scores[j] + score_part(last, j)
        share(j).start()
    for j in range(NZ):
        share(j).wait_recv()

    def softmax_of(i):
        n = c * half_g + i
        keep = soft_t[0, pl.ds(pl.multiple_of(n * SEATS, SEATS), SEATS), 0:1].astype(F32)
        parts = []
        top = None
        for j in range(NZ):
            s = inverse_temp * (scores[j, n] + scores_in[j, i])
            s = jnp.where(valid[j, 0:1, :] > 0, s, -1e30)
            parts.append(s)
            m = jnp.max(s, axis=1, keepdims=True)
            top = m if top is None else jnp.maximum(top, m)
        total = None
        exps = []
        for s in parts:
            e = jnp.exp(s - top)
            exps.append(e)
            t = jnp.sum(e, axis=1, keepdims=True)
            total = t if total is None else total + t
        for j in range(NZ):
            soft[j, n] = jnp.where(keep > 0, exps[j] / total, 0.0).astype(BF16)

    pieces = min(4, half_g)
    piece = half_g // pieces

    def give(i):
        part = pl.ds(c * half_g + i * piece, piece)
        return remote(soft.at[:, part, taken], soft.at[:, part, taken], give_s.at[i], give_r.at[i], (g, mate))

    for i in range(pieces):

        @pl.loop(i * piece, (i + 1) * piece, unroll=True)
        def _(n):
            softmax_of(n)

        give(i).start()
    my_lanes = pl.ds(pl.multiple_of(c * half, half), half)
    mate_lanes = pl.ds(pl.multiple_of((1 - c) * half, half), half)
    my_seats = pl.ds(c * half_g, half_g)

    @pl.loop(0, NZ)
    def _(j):
        soft_t[j, :, my_lanes] = soft[j, my_seats].reshape(half, rows).T

    for i in range(pieces):
        give(i).wait_recv()

    @pl.loop(0, NZ)
    def _(j):
        soft_t[j, :, mate_lanes] = soft[j, mate_seats].reshape(half, rows).T

    def q_of(k):
        return q_rows[k].reshape(rows, width)

    def term(k, j, first, size):
        return inverse_temp * jnp.dot(soft_t[j, pl.ds(first, size), :], q_of(k), preferred_element_type=F32)

    def blocks(x):
        return x.astype(BF16).reshape(x.shape[0] // SEATS, SEATS, width)

    def summed(k, i):
        src, dst, to = (
            (t2.at[k, lo, taken], ra.at[k, :, taken], up),
            (t2.at[k, hi, taken], rb.at[k, :, taken], down),
            (t1.at[k, hi, taken], rl.at[k, hi, taken], up),
            (t3.at[k, lo, taken], rr.at[k, lo, taken], down),
            (t1.at[k, lo, taken], rl.at[k, lo, taken], up),
            (t3.at[k, hi, taken], rr.at[k, hi, taken], down),
        )[i]
        return remote(src, dst, sum_s.at[k, i], sum_r.at[k, i], (g, to))

    def open_sums(k):
        t2[k] = blocks(term(k, 2, 0, rows))
        summed(k, 0).start()
        summed(k, 1).start()
        t1[k, hi] = blocks(term(k, 1, half, half))
        summed(k, 2).start()
        t3[k, lo] = blocks(term(k, 3, 0, half))
        summed(k, 3).start()

    def add_sums(k):
        summed(k, 0).wait_recv()
        t1[k, lo] = blocks(term(k, 1, 0, half) + ra[k].reshape(half, width).astype(F32))
        summed(k, 4).start()
        summed(k, 1).wait_recv()
        t3[k, hi] = blocks(term(k, 3, half, half) + rb[k].reshape(half, width).astype(F32))
        summed(k, 5).start()

    def query_part(k):
        acc = -p_all[k, 0].reshape(rows, width).astype(F32)
        for j in range(NZ):
            acc = acc + jnp.dot(soft[j].reshape(rows, rows), p_all[k, j].reshape(rows, width), preferred_element_type=F32)
        dq[k] = blocks(inverse_temp * acc)
        send_all(dq.at[k], back_q.at[k], back_s.at[0, k], back_r.at[0, k])
        back_q[k, g, 0:seats] = dq[k, g, 0:seats]

    def close_sums(k):
        own = inverse_temp * (
            jnp.dot(soft_t[0], q_of(k), preferred_element_type=F32) - q_of(k).astype(F32)
        )
        for i in (2, 3, 4, 5):
            summed(k, i).wait_recv()
        own = own + rl[k].reshape(rows, width).astype(F32) + rr[k].reshape(rows, width).astype(F32)
        dp[k] = blocks(own)
        send_all(dp.at[k], back_p.at[k], back_s.at[1, k], back_r.at[1, k])
        back_p[k, g, 0:seats] = dp[k, g, 0:seats]

    open_sums(0)
    query_part(0)
    open_sums(1)
    add_sums(0)
    query_part(1)

    @pl.loop(2, CHUNKS)
    def _(k):
        open_sums(k)
        add_sums(k - 1)
        query_part(k)
        close_sums(k - 2)

    add_sums(CHUNKS - 1)
    close_sums(CHUNKS - 2)
    close_sums(CHUNKS - 1)

    def outputs(k, which):
        out, o_ref = ((out_q, oq_ref), (out_p, op_ref))[which]
        cols = pl.ds(pl.multiple_of(c * half_d + k * width, width), width)
        return (
            pltpu.make_async_copy(out.at[k, c], o_ref.at[:, cols], keep_s.at[which, k]),
            remote(out.at[k, 1 - c], o_ref.at[:, cols], out_s.at[which, k], out_r.at[which, k], (g, mate)),
        )

    for which in range(2):
        back, out = ((back_q, out_q), (back_p, out_p))[which]

        @pl.loop(0, CHUNKS)
        def _(k):
            wait_all(back.at[k], back_r.at[which, k])
            part = jnp.dot(unplace[...], back[k].reshape(rows, width), preferred_element_type=F32)
            out[k] = part.astype(BF16).reshape(2, npairs, width)
            here, there = outputs(k, which)
            here.start()
            there.start()

    @pl.loop(0, CHUNKS)
    def _(k):
        wait_all(pay_p.at[k], place_s.at[0, k])
        wait_all(pay_q.at[k], place_s.at[1, k])
        wait_all(dq.at[k], back_s.at[0, k])
        wait_all(dp.at[k], back_s.at[1, k])
        for i in range(6):
            summed(k, i).wait_send()
        for which in range(2):
            here, there = outputs(k, which)
            here.wait()
            there.wait()

    wait_bytes(marks_out.at[pl.ds(0, n_group - 1)], mark_s.at[0])
    @pl.loop(RAW, CHUNKS)
    def _(k):
        for i in range(6):
            ring(k, i).wait_send()

    for i in range(6):
        raw(i).wait_send()
    for k in range(RAW):
        for j in range(NZ - 1):
            wait_all(raw_pay.at[k, j], raw_s.at[k, j])
    wait_bytes(tops.at[pl.ds(0, n_group - 1)], top_s)
    for copy in swaps + dest_copies + mark_ring + plane_copies:
        copy.wait_send()
    for j in range(NZ):
        share(j).wait_send()
    for i in range(pieces):
        give(i).wait_send()


def local(queries, passages, destination):
    n_group = lax.axis_size("grp")
    npairs, width_d = queries.shape
    half_d = width_d // 2
    width = half_d // CHUNKS
    rows = n_group * SEATS
    half = rows // 2
    half_g = n_group // 2
    drow = jnp.broadcast_to(destination.reshape(1, npairs), (8, npairs))
    dma = pltpu.SemaphoreType.DMA
    in_vmem = pl.BlockSpec(memory_space=pltpu.VMEM)
    anywhere = pl.BlockSpec(memory_space=pl.ANY)

    def vm(*shape, dtype=BF16):
        return pltpu.VMEM(shape, dtype)

    tile = (8, 128)
    payload = (CHUNKS, n_group, SEATS, width)
    def call(seats, collective_id):
        scratch = [
            vm(NZ, 2, 8, npairs, dtype=jnp.int32),
            vm(NZ, 2, npairs, RAW * width), vm(RAW, NZ - 1, n_group, SEATS, width),
            vm(2, npairs, half_d), vm(2, npairs, half_d),
            vm(rows, 2 * npairs), vm(2 * npairs, rows),
            vm(*payload), vm(*payload), vm(n_group, *tile, dtype=F32),
            vm(*tile, dtype=F32), vm(n_group, *tile, dtype=F32),
            vm(*tile, dtype=F32), vm(3, *tile, dtype=F32),
            vm(CHUNKS, NZ, n_group, SEATS, width), vm(*payload),
            vm(NZ, n_group, *tile, dtype=F32), vm(NZ, 8, rows, dtype=F32),
            vm(NZ, n_group, SEATS, rows, dtype=F32), vm(NZ, half_g, SEATS, rows, dtype=F32),
            vm(NZ, n_group, SEATS, rows), vm(NZ, rows, rows),
            vm(*payload),
            vm(*payload), vm(*payload), vm(*payload),
            vm(CHUNKS, half_g, SEATS, width), vm(CHUNKS, half_g, SEATS, width),
            vm(*payload), vm(*payload), vm(*payload),
            vm(*payload), vm(*payload),
            vm(CHUNKS, 2, npairs, width), vm(CHUNKS, 2, npairs, width),
            dma((4,)), dma((4,)), dma((4,)), dma((3,)), dma((3,)), dma((RAW, 3)), dma((RAW, 3)),
            dma(()), dma(()), dma((3,)), dma((3,)),
            dma((2, CHUNKS)), dma((2, CHUNKS)), dma((4,)), dma((4,)),
            dma((CHUNKS, 6)), dma((CHUNKS, 6)), dma((NZ,)), dma((NZ,)), dma((4,)), dma((4,)),
            dma((CHUNKS, 6)), dma((CHUNKS, 6)), dma((2, CHUNKS)), dma((2, CHUNKS)),
            dma((2, CHUNKS)), dma((2, CHUNKS)), dma((2, CHUNKS)),
        ]
        return pl.pallas_call(
            functools.partial(kernel, seats),
            out_shape=(
                jax.ShapeDtypeStruct((npairs, width_d), BF16),
                jax.ShapeDtypeStruct((npairs, width_d), BF16),
                jax.ShapeDtypeStruct(tile, F32),
            ),
            in_specs=[in_vmem, anywhere, anywhere],
            out_specs=(anywhere, anywhere, in_vmem),
            scratch_shapes=scratch,
            compiler_params=pltpu.CompilerParams(
                collective_id=collective_id, has_side_effects=True, vmem_limit_bytes=67043328
            ),
        )(drow, queries, passages)

    query_grads, passage_grads, top = call(FEW, 0)
    return lax.cond(
        top[0, 0] <= FEW, lambda: (query_grads, passage_grads), lambda: tuple(call(SEATS, 1)[:2])
    )


def solution(mesh):
    placed = (P(("grp", "dev"), None), P(("grp", "dev"), None), P(("grp", "dev"), None))
    return jax.shard_map(
        local,
        mesh=mesh,
        in_specs=placed,
        out_specs=(P(("grp", "dev"), None), P(("grp", "dev"), None)),
        check_vma=False,
    )
```

```python
import functools

import jax
import jax.numpy as jnp
from jax import lax
from jax.experimental import pallas as pl
from jax.experimental.pallas import tpu as pltpu
from jax.sharding import PartitionSpec as P

inverse_temp = 100.0
MESH = pl.DeviceIdType.MESH
SEATS = 32
FEW = 24
NZ = 4
CHUNKS = 8
RAW = 2
F32, BF16 = jnp.float32, jnp.bfloat16


def wait_bytes(ref, sem):
    pltpu.make_async_copy(ref, ref, sem).wait()


def remote(src, dst, s, r, to):
    return pltpu.make_async_remote_copy(
        src_ref=src, dst_ref=dst, send_sem=s, recv_sem=r, device_id=to, device_id_type=MESH
    )


def where_am_i():
    g = lax.axis_index("grp")
    d = lax.axis_index("dev")
    c = lax.rem(d, 2)
    z = lax.div(d, 2)
    up = lax.rem(z + 1, NZ) * 2 + c
    down = lax.rem(z + NZ - 1, NZ) * 2 + c
    far = lax.rem(z + 2, NZ) * 2 + c
    mate = z * 2 + (1 - c)
    return g, d, c, up, down, far, mate


def greet(n_group):
    g, d, c, up, down, far, mate = where_am_i()
    barrier = pltpu.get_barrier_semaphore()
    for to in (up, down, far, mate):
        pl.semaphore_signal(barrier, inc=1, device_id=(g, to), device_id_type=MESH)

    @pl.loop(1, n_group)
    def _(o):
        pl.semaphore_signal(barrier, inc=1, device_id=(lax.rem(g + o, n_group), d), device_id_type=MESH)

    return lambda: pl.semaphore_wait(barrier, n_group + 3)


def kernel(
    seats,
    drow_ref, q_ref, p_ref, oq_ref, op_ref, top_ref,
    dest, raw_x, raw_pay, xp, xq, place, unplace, pay_p, pay_q, marks_out, own_top, tops, plane_top, plane_tops,
    p_all, q_rows, marks, valid, scores, scores_in, soft, soft_t, dq, t1, t2, t3, ra, rb, rl, rr, dp,
    back_q, back_p, out_q, out_p,
    swap_s, swap_r, local_s, dest_s, dest_r, raw_s, raw_r, top_s, top_r, plane_s, plane_r,
    place_s, place_r, mark_s, mark_r, ring_s, ring_r, core_s, core_r, give_s, give_r,
    sum_s, sum_r, back_s, back_r, keep_s, out_s, out_r,
):
    n_group = p_all.shape[2]
    npairs, width_d = oq_ref.shape
    half_d = width_d // 2
    width = p_all.shape[4]
    rows = n_group * SEATS
    half_g = n_group // 2
    half = rows // 2
    g, d, c, up, down, far, mate = where_am_i()
    taken = pl.ds(0, seats)

    early = RAW * width
    first = pl.ds(pl.multiple_of(c * half_d, early), early)
    others = pl.ds(pl.multiple_of(c * half_d + early, early), half_d - early)
    mine = pl.ds(pl.multiple_of(c * half_d, half_d), half_d)
    mate_first = pl.ds(pl.multiple_of((1 - c) * half_d, early), early)
    mate_others = pl.ds(pl.multiple_of((1 - c) * half_d + early, early), half_d - early)
    theirs = pl.ds(pl.multiple_of((1 - c) * half_d, half_d), half_d)
    tail = pl.ds(early, half_d - early)
    own_copies = [
        pltpu.make_async_copy(drow_ref, dest.at[0, c], local_s.at[0]),
        pltpu.make_async_copy(p_ref.at[:, first], raw_x.at[0, c], local_s.at[1]),
        pltpu.make_async_copy(p_ref.at[:, others], xp.at[c, :, tail], local_s.at[2]),
        pltpu.make_async_copy(q_ref.at[:, mine], xq.at[c], local_s.at[3]),
    ]
    swaps = [
        remote(drow_ref, dest.at[0, c], swap_s.at[0], swap_r.at[0], (g, mate)),
        remote(p_ref.at[:, mate_first], raw_x.at[0, c], swap_s.at[1], swap_r.at[1], (g, mate)),
        remote(p_ref.at[:, mate_others], xp.at[c, :, tail], swap_s.at[2], swap_r.at[2], (g, mate)),
        remote(q_ref.at[:, theirs], xq.at[c], swap_s.at[3], swap_r.at[3], (g, mate)),
    ]
    ready = greet(n_group)
    for copy in own_copies:
        copy.start()
    if seats < SEATS:
        rest = slice(seats, SEATS)
        empty = jnp.zeros((n_group, SEATS - seats, width), BF16)

        @pl.loop(0, CHUNKS)
        def _(k):
            for j in range(NZ):
                p_all[k, j, :, rest, :] = empty
            for ref in (q_rows, back_q, back_p):
                ref[k, :, rest, :] = empty

    ready()

    def send_all(src, dst, s, r):
        @pl.loop(1, n_group)
        def _(o):
            to = lax.rem(g + o, n_group)
            remote(src.at[to, taken], dst.at[g, taken], s, r, (to, d)).start()

    def wait_all(ref, sem):
        wait_bytes(ref.at[pl.ds(0, n_group - 1), taken], sem)

    for copy in swaps:
        copy.start()

    def arrived(i):
        own_copies[i].wait()
        swaps[i].wait_recv()

    n2 = 2 * npairs
    i0 = lax.broadcasted_iota(jnp.int32, (n2, n2), 0)
    i1 = lax.broadcasted_iota(jnp.int32, (n2, n2), 1)

    def groups_of(j):
        group = jnp.concatenate([dest[j, 0, 0:1, :], dest[j, 1, 0:1, :]], axis=1)
        group = lax.shift_right_logical(group, jnp.full_like(group, 3))
        across = jnp.broadcast_to(group.astype(F32), (n2, n2)).T
        return group, across, group.astype(F32) == across

    def placing(group, same):
        rank_row = jnp.sum(jnp.where(same & (i0 < i1), 1.0, 0.0), axis=0, keepdims=True)
        slot_row = (group.astype(F32) * SEATS + rank_row).astype(jnp.int32)
        return jnp.where(lax.broadcasted_iota(jnp.int32, (rows, n2), 0) == slot_row, 1.0, 0.0).astype(BF16)

    dest_copies = [
        remote(dest.at[0], dest.at[j], dest_s.at[j - 1], dest_r.at[j - 1], (g, to))
        for j, to in ((1, down), (2, far), (3, up))
    ]

    def raw(i):
        src, dst, core, to = (
            (0, 3, 0, up), (0, 3, 1, up), (0, 1, 1, down), (0, 1, 0, down), (3, 2, 0, up), (1, 2, 1, down)
        )[i]
        return remote(raw_x.at[src, core], raw_x.at[dst, core], ring_s.at[0, i], ring_r.at[0, i], (g, to))

    arrived(0)
    arrived(1)
    for i in (0, 2, 1, 3):
        raw(i).start()
    for copy in dest_copies:
        copy.start()
    group, across, same = groups_of(0)
    place[...] = placing(group, same)

    def fill_from(placer, x, pay, into, s, r):
        part = jnp.dot(placer, x.reshape(n2, width), preferred_element_type=F32)
        pay[...] = part.astype(BF16).reshape(n_group, SEATS, width)
        send_all(pay, into, s, r)
        into[g, 0:seats] = pay[g, 0:seats]

    def columns(k):
        return pl.ds(k * width if isinstance(k, int) else pl.multiple_of(k * width, width), width)

    def fill_p(k):
        fill_from(
            place[...], xp[:, :, columns(k)], pay_p.at[k], p_all.at[k, 0], place_s.at[0, k], place_r.at[0, k]
        )

    def fill_q(k):
        fill_from(place[...], xq[:, :, columns(k)], pay_q.at[k], q_rows.at[k], place_s.at[1, k], place_r.at[1, k])

    def fill_own(k):
        fill_from(
            place[...], raw_x[0, :, :, columns(k)], pay_p.at[k], p_all.at[k, 0], place_s.at[0, k], place_r.at[0, k]
        )

    def fill_raw(j):
        group, _, same = groups_of(j)
        placer = placing(group, same)
        for k in range(RAW):
            fill_from(
                placer, raw_x[j, :, :, columns(k)], raw_pay.at[k, j - 1], p_all.at[k, j],
                raw_s.at[k, j - 1], raw_r.at[k, j - 1],
            )

    arrived(2)
    fill_p(2)
    raw(0).wait_recv()
    raw(4).start()
    raw(2).wait_recv()
    raw(5).start()

    @pl.loop(3, 5)
    def _(k):
        fill_p(k)

    count = jnp.sum(
        jnp.where(lax.broadcasted_iota(jnp.int32, (n_group, n2), 0) == group, 1.0, 0.0), axis=1, keepdims=True
    )
    lane = lax.broadcasted_iota(jnp.int32, (n_group, 128), 1) - lax.rem(g, 4) * SEATS
    flags = jnp.where((lane >= 0) & (lane < count.astype(jnp.int32)), 1.0, 0.0)
    for i in range(n_group):
        marks_out[i] = jnp.broadcast_to(flags[i : i + 1], (8, 128))
    marks[0, g] = marks_out[g]
    own_top[...] = jnp.broadcast_to(jnp.max(count, axis=0, keepdims=True), (8, 128))
    tops[g] = own_top[...]

    @pl.loop(1, n_group)
    def _(o):
        to = lax.rem(g + o, n_group)
        remote(marks_out.at[to], marks.at[0, g], mark_s.at[0], mark_r.at[0], (to, d)).start()
        remote(own_top, tops.at[g], top_s, top_r, (to, d)).start()

    arrived(3)
    fill_q(2)

    lo, hi = pl.ds(0, half_g), pl.ds(half_g, half_g)

    def ring(k, i):
        own, above, beyond, below = (p_all.at[k, j] for j in range(4))
        src, dst, part, to = (
            (own, below, lo, up),
            (own, below, hi, up),
            (own, above, hi, down),
            (own, above, lo, down),
            (below, beyond, lo, up),
            (above, beyond, hi, down),
        )[i]
        return remote(src.at[part, taken], dst.at[part, taken], ring_s.at[k, i], ring_r.at[k, i], (g, to))

    def score_part(k, j):
        return lax.dot_general(
            q_rows[k].reshape(rows, width), p_all[k, j].reshape(rows, width),
            (((1,), (1,)), ((), ())), preferred_element_type=F32,
        ).reshape(n_group, SEATS, rows)

    def start_ring(k):
        wait_all(p_all.at[k, 0], place_r.at[0, k])
        for i in (0, 2, 1, 3):
            ring(k, i).start()

    def pass_on(k):
        ring(k, 0).wait_recv()
        ring(k, 4).start()
        ring(k, 2).wait_recv()
        ring(k, 5).start()

    def add_scores(k):
        wait_all(q_rows.at[k], place_r.at[1, k])
        if isinstance(k, int) and k < RAW:
            wait_all(p_all.at[k, 0], place_r.at[0, k])
            for j in range(1, NZ):
                wait_all(p_all.at[k, j], raw_r.at[k, j - 1])
        else:
            for i in (1, 3, 4, 5):
                ring(k, i).wait_recv()

        @pl.loop(0, NZ)
        def _(j):
            scores[j] = scores[j] + score_part(k, j)

    mark_ring = [
        remote(marks.at[0], marks.at[3], mark_s.at[1], mark_r.at[1], (g, up)),
        remote(marks.at[0], marks.at[1], mark_s.at[2], mark_r.at[2], (g, down)),
        remote(marks.at[0], marks.at[2], mark_s.at[3], mark_r.at[3], (g, far)),
    ]

    plane_copies = [
        remote(plane_top, plane_tops.at[i], plane_s.at[i], plane_r.at[i], (g, to))
        for i, to in enumerate((up, down, far))
    ]

    start_ring(2)
    fill_p(5)
    fill_q(3)
    fill_p(6)
    wait_bytes(marks.at[0, pl.ds(0, n_group - 1)], mark_r.at[0])
    for copy in mark_ring:
        copy.start()
    scores[...] = jnp.zeros_like(scores)
    soft[...] = jnp.zeros_like(soft)
    rank_col = jnp.sum(jnp.where(same & (i1 < i0), 1.0, 0.0), axis=1, keepdims=True)
    slot_col = (across[:, 0:1] * SEATS + rank_col).astype(jnp.int32)
    unplace[...] = jnp.where(
        lax.broadcasted_iota(jnp.int32, (n2, rows), 1) == slot_col, 1.0, 0.0
    ).astype(BF16)

    start_ring(3)
    pass_on(2)
    fill_p(7)
    fill_q(4)
    for copy in mark_ring:
        copy.wait_recv()
    for j in range(NZ):
        pieces = []
        for first_mark in range(0, n_group, 4):
            flag = marks[j, first_mark, 0:1, :]
            for i in range(first_mark + 1, min(first_mark + 4, n_group)):
                flag = flag + marks[j, i, 0:1, :]
            pieces.append(flag)
        flag = pieces[0] if len(pieces) == 1 else jnp.concatenate(pieces, axis=1)
        valid[j] = jnp.broadcast_to(flag[:, :rows], (8, rows))
    wait_bytes(tops.at[pl.ds(0, n_group - 1)], top_r)
    top = tops[0]
    for i in range(1, n_group):
        top = jnp.maximum(top, tops[i])
    plane_top[...] = top
    for copy in plane_copies:
        copy.start()
    soft_t[0, :, 0:128] = jnp.broadcast_to(valid[0, 0:1, :], (128, rows)).T.astype(BF16)
    for copy in dest_copies:
        copy.wait_recv()
    for i in (1, 3, 4, 5):
        raw(i).wait_recv()

    for k in range(RAW):
        fill_own(k)
        fill_q(k)

    @pl.loop(4, 7)
    def _(step):
        start_ring(step)
        pass_on(step - 1)
        fill_raw(step - 3)
        fill_q(step + 1)
        add_scores(step - 2)

    start_ring(7)
    pass_on(6)
    add_scores(5)
    for copy in plane_copies:
        copy.wait_recv()
    top_ref[...] = jnp.maximum(
        jnp.maximum(plane_top[...], plane_tops[0]), jnp.maximum(plane_tops[1], plane_tops[2])
    )
    pass_on(7)
    add_scores(0)
    add_scores(1)
    add_scores(6)

    mate_seats = pl.ds((1 - c) * half_g, half_g)

    def share(j):
        return remote(scores.at[j, mate_seats, taken], scores_in.at[j, :, taken], core_s.at[j], core_r.at[j], (g, mate))

    last = CHUNKS - 1
    wait_all(q_rows.at[last], place_r.at[1, last])
    for j, needs in ((0, ()), (3, (1,)), (1, (3,)), (2, (4, 5))):
        for i in needs:
            ring(last, i).wait_recv()
        scores[j] = scores[j] + score_part(last, j)
        share(j).start()
    for j in range(NZ):
        share(j).wait_recv()

    def softmax_of(i):
        n = c * half_g + i
        keep = soft_t[0, pl.ds(pl.multiple_of(n * SEATS, SEATS), SEATS), 0:1].astype(F32)
        parts = []
        top = None
        for j in range(NZ):
            s = inverse_temp * (scores[j, n] + scores_in[j, i])
            s = jnp.where(valid[j, 0:1, :] > 0, s, -1e30)
            parts.append(s)
            m = jnp.max(s, axis=1, keepdims=True)
            top = m if top is None else jnp.maximum(top, m)
        total = None
        exps = []
        for s in parts:
            e = jnp.exp(s - top)
            exps.append(e)
            t = jnp.sum(e, axis=1, keepdims=True)
            total = t if total is None else total + t
        for j in range(NZ):
            soft[j, n] = jnp.where(keep > 0, exps[j] / total, 0.0).astype(BF16)

    pieces = min(4, half_g)
    piece = half_g // pieces

    def give(i):
        part = pl.ds(c * half_g + i * piece, piece)
        return remote(soft.at[:, part, taken], soft.at[:, part, taken], give_s.at[i], give_r.at[i], (g, mate))

    for i in range(pieces):

        @pl.loop(i * piece, (i + 1) * piece, unroll=True)
        def _(n):
            softmax_of(n)

        give(i).start()
    my_lanes = pl.ds(pl.multiple_of(c * half, half), half)
    mate_lanes = pl.ds(pl.multiple_of((1 - c) * half, half), half)
    my_seats = pl.ds(c * half_g, half_g)

    @pl.loop(0, NZ)
    def _(j):
        soft_t[j, :, my_lanes] = soft[j, my_seats].reshape(half, rows).T

    for i in range(pieces):
        give(i).wait_recv()

    @pl.loop(0, NZ)
    def _(j):
        soft_t[j, :, mate_lanes] = soft[j, mate_seats].reshape(half, rows).T

    def q_of(k):
        return q_rows[k].reshape(rows, width)

    def term(k, j, first, size):
        return inverse_temp * jnp.dot(soft_t[j, pl.ds(first, size), :], q_of(k), preferred_element_type=F32)

    def blocks(x):
        return x.astype(BF16).reshape(x.shape[0] // SEATS, SEATS, width)

    def summed(k, i):
        src, dst, to = (
            (t2.at[k, lo, taken], ra.at[k, :, taken], up),
            (t2.at[k, hi, taken], rb.at[k, :, taken], down),
            (t1.at[k, hi, taken], rl.at[k, hi, taken], up),
            (t3.at[k, lo, taken], rr.at[k, lo, taken], down),
            (t1.at[k, lo, taken], rl.at[k, lo, taken], up),
            (t3.at[k, hi, taken], rr.at[k, hi, taken], down),
        )[i]
        return remote(src, dst, sum_s.at[k, i], sum_r.at[k, i], (g, to))

    def open_sums(k):
        t2[k] = blocks(term(k, 2, 0, rows))
        summed(k, 0).start()
        summed(k, 1).start()
        t1[k, hi] = blocks(term(k, 1, half, half))
        summed(k, 2).start()
        t3[k, lo] = blocks(term(k, 3, 0, half))
        summed(k, 3).start()

    def add_sums(k):
        summed(k, 0).wait_recv()
        t1[k, lo] = blocks(term(k, 1, 0, half) + ra[k].reshape(half, width).astype(F32))
        summed(k, 4).start()
        summed(k, 1).wait_recv()
        t3[k, hi] = blocks(term(k, 3, half, half) + rb[k].reshape(half, width).astype(F32))
        summed(k, 5).start()

    def query_part(k):
        acc = -p_all[k, 0].reshape(rows, width).astype(F32)
        for j in range(NZ):
            acc = acc + jnp.dot(soft[j].reshape(rows, rows), p_all[k, j].reshape(rows, width), preferred_element_type=F32)
        dq[k] = blocks(inverse_temp * acc)
        send_all(dq.at[k], back_q.at[k], back_s.at[0, k], back_r.at[0, k])
        back_q[k, g, 0:seats] = dq[k, g, 0:seats]

    def close_sums(k):
        own = inverse_temp * (
            jnp.dot(soft_t[0], q_of(k), preferred_element_type=F32) - q_of(k).astype(F32)
        )
        for i in (2, 3, 4, 5):
            summed(k, i).wait_recv()
        own = own + rl[k].reshape(rows, width).astype(F32) + rr[k].reshape(rows, width).astype(F32)
        dp[k] = blocks(own)
        send_all(dp.at[k], back_p.at[k], back_s.at[1, k], back_r.at[1, k])
        back_p[k, g, 0:seats] = dp[k, g, 0:seats]

    def outputs(k, which):
        out, o_ref = ((out_q, oq_ref), (out_p, op_ref))[which]
        cols = pl.ds(pl.multiple_of(c * half_d + k * width, width), width)
        return (
            pltpu.make_async_copy(out.at[k, c], o_ref.at[:, cols], keep_s.at[which, k]),
            remote(out.at[k, 1 - c], o_ref.at[:, cols], out_s.at[which, k], out_r.at[which, k], (g, mate)),
        )

    def finish(k, which):
        back, out = ((back_q, out_q), (back_p, out_p))[which]
        wait_all(back.at[k], back_r.at[which, k])
        part = jnp.dot(unplace[...], back[k].reshape(rows, width), preferred_element_type=F32)
        out[k] = part.astype(BF16).reshape(2, npairs, width)
        here, there = outputs(k, which)
        here.start()
        there.start()

    open_sums(0)
    query_part(0)
    open_sums(1)
    add_sums(0)
    query_part(1)

    @pl.loop(2, 4)
    def _(k):
        open_sums(k)
        add_sums(k - 1)
        query_part(k)
        close_sums(k - 2)

    @pl.loop(4, CHUNKS)
    def _(k):
        open_sums(k)
        add_sums(k - 1)
        query_part(k)
        close_sums(k - 2)
        finish(k - 4, 0)

    add_sums(CHUNKS - 1)
    close_sums(CHUNKS - 2)
    finish(4, 0)
    finish(5, 0)
    close_sums(CHUNKS - 1)
    finish(6, 0)
    finish(7, 0)

    @pl.loop(0, CHUNKS)
    def _(k):
        finish(k, 1)

    @pl.loop(0, CHUNKS)
    def _(k):
        wait_all(pay_p.at[k], place_s.at[0, k])
        wait_all(pay_q.at[k], place_s.at[1, k])
        wait_all(dq.at[k], back_s.at[0, k])
        wait_all(dp.at[k], back_s.at[1, k])
        for i in range(6):
            summed(k, i).wait_send()
        for which in range(2):
            here, there = outputs(k, which)
            here.wait()
            there.wait()

    wait_bytes(marks_out.at[pl.ds(0, n_group - 1)], mark_s.at[0])
    @pl.loop(RAW, CHUNKS)
    def _(k):
        for i in range(6):
            ring(k, i).wait_send()

    for i in range(6):
        raw(i).wait_send()
    for k in range(RAW):
        for j in range(NZ - 1):
            wait_all(raw_pay.at[k, j], raw_s.at[k, j])
    wait_bytes(tops.at[pl.ds(0, n_group - 1)], top_s)
    for copy in swaps + dest_copies + mark_ring + plane_copies:
        copy.wait_send()
    for j in range(NZ):
        share(j).wait_send()
    for i in range(pieces):
        give(i).wait_send()


def local(queries, passages, destination):
    n_group = lax.axis_size("grp")
    npairs, width_d = queries.shape
    half_d = width_d // 2
    width = half_d // CHUNKS
    rows = n_group * SEATS
    half = rows // 2
    half_g = n_group // 2
    drow = destination.reshape(1, npairs)
    dma = pltpu.SemaphoreType.DMA
    in_vmem = pl.BlockSpec(memory_space=pltpu.VMEM)
    anywhere = pl.BlockSpec(memory_space=pl.ANY)

    def vm(*shape, dtype=BF16):
        return pltpu.VMEM(shape, dtype)

    tile = (8, 128)
    payload = (CHUNKS, n_group, SEATS, width)
    def call(seats, collective_id):
        scratch = [
            vm(NZ, 2, 1, npairs, dtype=jnp.int32),
            vm(NZ, 2, npairs, RAW * width), vm(RAW, NZ - 1, n_group, SEATS, width),
            vm(2, npairs, half_d), vm(2, npairs, half_d),
            vm(rows, 2 * npairs), vm(2 * npairs, rows),
            vm(*payload), vm(*payload), vm(n_group, *tile, dtype=F32),
            vm(*tile, dtype=F32), vm(n_group, *tile, dtype=F32),
            vm(*tile, dtype=F32), vm(3, *tile, dtype=F32),
            vm(CHUNKS, NZ, n_group, SEATS, width), vm(*payload),
            vm(NZ, n_group, *tile, dtype=F32), vm(NZ, 8, rows, dtype=F32),
            vm(NZ, n_group, SEATS, rows, dtype=F32), vm(NZ, half_g, SEATS, rows, dtype=F32),
            vm(NZ, n_group, SEATS, rows), vm(NZ, rows, rows),
            vm(*payload),
            vm(*payload), vm(*payload), vm(*payload),
            vm(CHUNKS, half_g, SEATS, width), vm(CHUNKS, half_g, SEATS, width),
            vm(*payload), vm(*payload), vm(*payload),
            vm(*payload), vm(*payload),
            vm(CHUNKS, 2, npairs, width), vm(CHUNKS, 2, npairs, width),
            dma((4,)), dma((4,)), dma((4,)), dma((3,)), dma((3,)), dma((RAW, 3)), dma((RAW, 3)),
            dma(()), dma(()), dma((3,)), dma((3,)),
            dma((2, CHUNKS)), dma((2, CHUNKS)), dma((4,)), dma((4,)),
            dma((CHUNKS, 6)), dma((CHUNKS, 6)), dma((NZ,)), dma((NZ,)), dma((4,)), dma((4,)),
            dma((CHUNKS, 6)), dma((CHUNKS, 6)), dma((2, CHUNKS)), dma((2, CHUNKS)),
            dma((2, CHUNKS)), dma((2, CHUNKS)), dma((2, CHUNKS)),
        ]
        return pl.pallas_call(
            functools.partial(kernel, seats),
            out_shape=(
                jax.ShapeDtypeStruct((npairs, width_d), BF16),
                jax.ShapeDtypeStruct((npairs, width_d), BF16),
                jax.ShapeDtypeStruct(tile, F32),
            ),
            in_specs=[in_vmem, anywhere, anywhere],
            out_specs=(anywhere, anywhere, in_vmem),
            scratch_shapes=scratch,
            compiler_params=pltpu.CompilerParams(
                collective_id=collective_id, has_side_effects=True, vmem_limit_bytes=67043328
            ),
        )(drow, queries, passages)

    query_grads, passage_grads, top = call(FEW, 0)
    return lax.cond(
        top[0, 0] <= FEW, lambda: (query_grads, passage_grads), lambda: tuple(call(SEATS, 1)[:2])
    )


def solution(mesh):
    placed = (P(("grp", "dev"), None), P(("grp", "dev"), None), P(("grp", "dev"), None))
    return jax.shard_map(
        local,
        mesh=mesh,
        in_specs=placed,
        out_specs=(P(("grp", "dev"), None), P(("grp", "dev"), None)),
        check_vma=False,
    )
```
